32 devices in a mesh: aux: 8 (over y, x, core), orb: 4 (over z).
Axes of the slice: x: 2, y: 2, z: 4, core: 2. Of those that a mesh axis runs over, the one named last changes fastest.
Arguments:
- band_pattern: int32 [64, 4], P('aux'), may hold values 0 or 1
- density_in: bfloat16 [64, 4, 128, 128], P('aux', 'orb')
- field_terms: bfloat16 [2, 64, 4, 128, 128], P(None, 'aux', 'orb'), may hold values from -3 to 3
- fit_blocks: int32 [1], replicated, may hold values from 0 to 63
- tensor: bfloat16 [1, 3072, 4, 16384], P(None, 'aux', 'orb'), may hold values from -0.0234375 to 0.0234375
- metric_inv: float32 [1, 3072, 3072], P(None, 'aux')
Outputs:
- response: bfloat16 [2, 64, 4, 128, 128], P(None, 'aux', 'orb')
- coefficients: float32 [1, 2, 3072], P(None, None, 'aux')
The draws below stay inside these ranges and needn't reach their ends.
All inputs are finite; a program needn't handle non-finite values. No bound on the sum of `band_pattern` on one device may be relied on, other than what follows from the above.
Results may differ from the reference program's by a relative error of at most 0.0055.
Values may be sent and summed in bfloat16 or wider, within the bound.
No kernel may reach another device: no remote copies, remote signals or barrier semaphores. Data moves between devices by JAX's collectives and lax.ppermute only.
A program may use at most 192 MiB of HBM per device.

```python
import math
import jax
import jax.numpy as jnp
from jax import lax

BLK = 128
FIELDS = 2
NFIT = 1
NAUX = 3072
SLOTS = 4
NBLK = 64


def draw_density_in(key, part):
    full_shape = (NBLK, SLOTS, BLK, BLK)
    spread = 0.6 / math.sqrt(SLOTS * BLK)
    random_part = jax.random.normal(key, full_shape, jnp.float32) * spread
    slot_flag = (jnp.arange(SLOTS) == SLOTS // 2).astype(jnp.float32)[None, :, None, None]
    diagonal = slot_flag * jnp.eye(BLK, dtype=jnp.float32)[None, None] * 0.5
    return (random_part + diagonal).astype(jnp.bfloat16)


def draw_metric_inv(key, part):
    full_shape = (NFIT, NAUX, NAUX)
    spread = 0.5 / math.sqrt(NAUX)
    random_part = jax.random.normal(key, full_shape, jnp.float32) * spread
    return random_part + jnp.eye(NAUX, dtype=jnp.float32)[None]


def plant(result, stream_key, low, high):
    longest = result.shape.index(max(result.shape))
    spots = []
    for shift in (0, 1):
        where = [jax.random.randint(jax.random.fold_in(stream_key, axis), (), 0, length) for axis, length in enumerate(result.shape)]
        where[longest] = (where[longest] + shift) % result.shape[longest]
        spots.append(tuple(where))
    return result.at[spots[0]].set(low).at[spots[1]].set(high)


def steps_of(key, extent, cuts, smallest, top_value):
    factor_of = 1.0
    for dim, shards_of in cuts:
        heights = jax.random.uniform(jax.random.fold_in(jax.random.fold_in(key, 6), dim), (shards_of,), jnp.float32, smallest / len(cuts), top_value / len(cuts))
        factor_of = factor_of * jnp.repeat(jnp.exp(heights), extent[dim] // shards_of).reshape((-1,) + (1,) * (len(extent) - 1 - dim))
    return factor_of


def bell_draw(rng, shape, width, bound, cuts=(), held_as=jnp.bfloat16):
    entries = jax.random.normal(rng, shape, jnp.float32) * width
    if len(cuts) > 0:
        entries = steps_of(rng, shape, cuts, -0.22, 0.18) * entries
    return jnp.clip(entries, min=-bound, max=bound).astype(held_as)


def setup_inputs(seed: int = 0) -> dict:
    arg_keys = jax.random.split(jax.random.key(seed), 7)
    band_pattern = plant((jax.random.randint(arg_keys[0], (NBLK, SLOTS), 0, 4) < 3).astype(jnp.int32), jax.random.fold_in(arg_keys[0], 1), 0, 1)
    density_in = draw_density_in(jax.random.fold_in(arg_keys[6], 71), 0)
    field_terms = bell_draw(arg_keys[2], (FIELDS, NBLK, SLOTS, BLK, BLK), 0.5, 3.0, ((1, 8), (2, 4)))
    fit_blocks = jax.random.randint(arg_keys[3], (NFIT,), 0, NBLK).astype(jnp.int32)
    tensor = bell_draw(arg_keys[4], (NFIT, NAUX, SLOTS, BLK * BLK), (SLOTS * BLK * BLK) ** -0.5, 0.0234375, ((1, 8), (2, 4)))
    metric_inv = draw_metric_inv(jax.random.fold_in(arg_keys[6], 71), 0)
    return {"band_pattern": band_pattern, "density_in": density_in, "field_terms": field_terms, "fit_blocks": fit_blocks, "tensor": tensor, "metric_inv": metric_inv}


def slide_slots(blocks, offset):
    slot_count = blocks.shape[2]
    if offset >= 0:
        padded = jnp.pad(blocks, ((0, 0), (0, 0), (offset, 0), (0, 0), (0, 0)))
        return padded[:, :, :slot_count]
    padded = jnp.pad(blocks, ((0, 0), (0, 0), (0, -offset), (0, 0), (0, 0)))
    return padded[:, :, -offset:-offset + slot_count]


def band_product(factor_left, factor_right):
    total_rows = factor_left.shape[1]
    slot_count = factor_left.shape[2]
    half_band = slot_count // 2
    padded = jnp.pad(factor_right, ((0, 0), (half_band, half_band), (0, 0), (0, 0), (0, 0)))
    lead_count = max(factor_left.shape[0], factor_right.shape[0])
    total = jnp.zeros((lead_count, total_rows, slot_count, factor_left.shape[3], factor_right.shape[4]), jnp.float32)
    for stride in range(slot_count):
        source = slide_slots(padded[:, stride:stride + total_rows], stride - half_band)
        factor = factor_left[:, :, stride:stride + 1].astype(jnp.float32)
        total = total + jnp.matmul(factor, source.astype(jnp.float32))
    return total


def band_keep(band_pattern):
    total_rows, slot_count = band_pattern.shape
    half_band = slot_count // 2
    row_ids = jnp.arange(total_rows, dtype=jnp.int32)[:, None]
    columns = row_ids + jnp.arange(slot_count, dtype=jnp.int32)[None, :] - half_band
    return (band_pattern == 1) & (columns >= 0) & (columns < total_rows)


def reference(band_pattern, density_in, field_terms, fit_blocks, tensor, metric_inv):
    keep_mask = band_keep(band_pattern)[None, :, :, None, None]
    zero_half = jnp.zeros((), jnp.bfloat16)
    density = jnp.where(keep_mask, density_in[None], zero_half)
    perturbed = jnp.where(keep_mask, field_terms, zero_half)
    density_sq = jnp.where(keep_mask, band_product(density, density), 0.0).astype(jnp.bfloat16)
    first_sum = band_product(density, perturbed) + band_product(perturbed, density)
    first_order = jnp.where(keep_mask, first_sum, 0.0).astype(jnp.bfloat16)
    second = band_product(density_sq, first_order) + band_product(first_order, density_sq)
    response = jnp.where(keep_mask, 2.0 * first_order.astype(jnp.float32) - second, 0.0).astype(jnp.bfloat16)
    fit_pairs = response[:, fit_blocks]
    flat_blocks = fit_pairs.reshape(fit_pairs.shape[0], fit_pairs.shape[1], -1)
    sums_list = []
    for fit_index in range(fit_pairs.shape[1]):
        integrals = tensor[fit_index].reshape(tensor.shape[1], -1)
        sums_list.append(jnp.dot(flat_blocks[:, fit_index], integrals.T, preferred_element_type=jnp.float32))
    fit_sums = jnp.stack(sums_list, 0)
    coefficients = jnp.einsum("fpq,fkq->fkp", metric_inv, fit_sums, precision=lax.Precision.HIGHEST)
    return response, coefficients
```

```python
import functools

import jax
import jax.numpy as jnp
from jax import lax
from jax.experimental import pallas as pl
from jax.experimental.pallas import tpu as pltpu
from jax.sharding import PartitionSpec as P


ANY = pl.BlockSpec(memory_space=pl.ANY)
SMEM = pl.BlockSpec(memory_space=pltpu.SMEM)
VMEM = pl.BlockSpec(memory_space=pltpu.VMEM)


def band_keep(band_pattern, first_row, total_rows):
    slot_count = band_pattern.shape[1]
    half_band = slot_count // 2
    row_ids = first_row + jnp.arange(band_pattern.shape[0], dtype=jnp.int32)[:, None]
    columns = row_ids + jnp.arange(slot_count, dtype=jnp.int32)[None, :] - half_band
    return (band_pattern == 1) & (columns >= 0) & (columns < total_rows)


def swap_pairs(count, distance):
    return [(i, i ^ distance) for i in range(count)]


def after(value, *others):
    return lax.optimization_barrier((value,) + others)[0]


def band_terms(slots, half, left, low, high, left_slots, sink):
    for first in range(left_slots[0], left_slots[1], 2):
        pair = [t for t in (first, first + 1) if t < left_slots[1]]
        hits = {t: [s for s in range(slots) if low <= s - t + half < high] for t in pair}
        pair = [t for t in pair if hits[t]]
        if not pair:
            continue
        span = range(min(hits[t][0] for t in pair), max(hits[t][-1] for t in pair) + 1)
        rows = []
        for t in pair:
            head, tail = hits[t][0] - span[0], span[-1] - hits[t][-1]
            rows.append((t, hits[t][0] - t + half, hits[t][-1] - t + half + 1, head, tail))
        sink(left(pair), rows, span)


def mid_kernel(
    slots, count_rows, fields, plan, scal, keep, *refs
):
    half = slots // 2
    blk = refs[0].shape[-1]
    n_in = plan["inputs"]
    ins, rest = refs[:n_in], refs[n_in:]
    outs, rest = rest[:slots], rest[slots:]
    fits, rest = rest[:slots], rest[slots:]
    dens, pert, square, order, sems = rest
    mid_rows = count_rows + 2 * half - 1
    middle, is_a, fit_row, owner = scal[0], scal[1], scal[2], scal[3]

    def cols(slot, width=1):
        return pl.ds(slot * blk, width * blk)

    def wide(ref, index, row, low, high, head, tail):
        parts = []
        zero = lambda n: jnp.zeros((blk, n * blk), jnp.bfloat16)
        if head:
            parts.append(zero(head))
        parts.append(ref[index + (row, slice(None), cols(low, high - low))])
        if tail:
            parts.append(zero(tail))
        return parts[0] if len(parts) == 1 else jnp.concatenate(parts, 1)

    def dot(a, b):
        return jnp.dot(a, b, preferred_element_type=jnp.float32)

    def body(side_is_a):
        copies = []
        for kind, field, distance, source, start, size, row in plan["moves"]:
            near = (half - 1 - distance) if side_is_a else (half + distance)
            far = (half + distance) if side_is_a else (half - 1 - distance)
            src = ins[source].at[pl.ds(start, size)]
            if kind == "side":
                dst = dens.at[pl.ds(row, size), :, cols(near)]
            elif kind == "other":
                dst = dens.at[pl.ds(row, size), :, cols(far)]
            else:
                local = near if side_is_a else near - half
                dst = pert.at[field, pl.ds(row, size), :, cols(local)]
            copies.append(pltpu.make_async_copy(src, dst, sems.at[len(copies)]))
        for copy in copies:
            copy.start()
        for copy in copies:
            copy.wait()
        base = 0 if side_is_a else half

        def add(total, field, span, value, lanes):
            for place, s in enumerate(span):
                part = value[:, (lanes + place) * blk : (lanes + place + 1) * blk]
                key = (field, s)
                total[key] = total[key] + part if key in total else part

        def first_step(j, carry):
            total = {}

            def left_dens(pair):
                return dens[j + half, :, cols(pair[0], len(pair))]

            def sink_square(lhs, rows, span):
                rhs = jnp.concatenate(
                    [wide(dens, (), j + t, lo, hi, head, tail) for t, lo, hi, head, tail in rows], 0
                )
                add(total, -1, span, dot(lhs, rhs), 0)

            band_terms(slots, half, left_dens, 0, slots, (0, slots), sink_square)

            def sink_right(lhs, rows, span):
                panels = []
                for field in range(fields):
                    panels.append(
                        jnp.concatenate(
                            [
                                wide(pert, (field,), j + t, lo - base, hi - base, head, tail)
                                for t, lo, hi, head, tail in rows
                            ],
                            0,
                        )
                    )
                value = dot(lhs, jnp.concatenate(panels, 1))
                for field in range(fields):
                    add(total, field, span, value, field * len(span))

            band_terms(slots, half, left_dens, base, base + half, (0, slots), sink_right)

            def left_pert(pair):
                return jnp.concatenate(
                    [pert[field, j + half, :, cols(pair[0] - base, len(pair))] for field in range(fields)], 0
                )

            def sink_left(lhs, rows, span):
                rhs = jnp.concatenate(
                    [wide(dens, (), j + t, lo, hi, head, tail) for t, lo, hi, head, tail in rows], 0
                )
                value = dot(lhs, rhs)
                for field in range(fields):
                    add(total, field, span, value[field * blk : (field + 1) * blk], 0)

            band_terms(slots, half, left_pert, 0, slots, (base, base + half), sink_left)
            for s in range(slots):
                kept = keep[j, s] != 0
                for field in range(-1, fields):
                    value = total.get((field, s), jnp.zeros((blk, blk), jnp.float32))
                    value = jnp.where(kept, value, 0.0).astype(jnp.bfloat16)
                    if field < 0:
                        square[j, :, cols(s)] = value
                    else:
                        order[field, j, :, cols(s)] = value
            return carry

        lax.fori_loop(0, mid_rows, first_step, 0)

        def second_step(i, carry):
            total = {}
            j = i + half

            def left_square(pair):
                return square[j, :, cols(pair[0], len(pair))]

            def sink_right(lhs, rows, span):
                panels = [
                    jnp.concatenate(
                        [wide(order, (field,), i + t, lo, hi, head, tail) for t, lo, hi, head, tail in rows], 0
                    )
                    for field in range(fields)
                ]
                value = dot(lhs, jnp.concatenate(panels, 1))
                for field in range(fields):
                    add(total, field, span, value, field * len(span))

            band_terms(slots, half, left_square, 0, slots, (0, slots), sink_right)

            def left_order(pair):
                return jnp.concatenate(
                    [order[field, j, :, cols(pair[0], len(pair))] for field in range(fields)], 0
                )

            def sink_left(lhs, rows, span):
                rhs = jnp.concatenate(
                    [wide(square, (), i + t, lo, hi, head, tail) for t, lo, hi, head, tail in rows], 0
                )
                value = dot(lhs, rhs)
                for field in range(fields):
                    add(total, field, span, value[field * blk : (field + 1) * blk], 0)

            band_terms(slots, half, left_order, 0, slots, (0, slots), sink_left)
            for s in range(slots):
                kept = keep[j, s] != 0
                step = (s - (half - 1)) % slots if side_is_a else (half - s) % slots
                for field in range(fields):
                    twice = 2.0 * order[field, j, :, cols(s)].astype(jnp.float32)
                    value = jnp.where(kept, twice - total[(field, s)], 0.0)
                    outs[step][field, i] = value.astype(jnp.bfloat16)
            return carry

        lax.fori_loop(0, count_rows, second_step, 0)
        for step in range(slots):
            for field in range(fields):
                value = outs[step][field, fit_row].astype(jnp.float32)
                fits[step][field] = jnp.where(owner != 0, value, 0.0).astype(jnp.bfloat16)

    @pl.when((middle != 0) & (is_a != 0))
    def _():
        body(True)

    @pl.when((middle != 0) & (is_a == 0))
    def _():
        body(False)

    @pl.when(middle == 0)
    def _():
        outs[0][...] = jnp.zeros_like(outs[0])
        fits[0][...] = jnp.zeros_like(fits[0])


def sums_kernel(flat, tensor, out, total):
    @pl.when(pl.program_id(0) == 0)
    def _():
        total[...] = jnp.zeros_like(total)

    total[...] += lax.dot_general(
        flat[...], tensor[...], (((1,), (1,)), ((), ())), preferred_element_type=jnp.float32
    )

    @pl.when(pl.program_id(0) == pl.num_programs(0) - 1)
    def _():
        out[...] = total[...]


def metric_kernel(sums, metric, out):
    groups, fields, width = sums.shape
    rows = out.shape[1]
    lanes = 128
    totals = [jnp.zeros((rows, lanes), jnp.float32) for _ in range(fields)]
    full = [
        jnp.concatenate([sums[group, field : field + 1, :] for group in range(groups)], 1)
        for field in range(fields)
    ]
    for start in range(0, groups * width, lanes):
        tile = metric[:, start : start + lanes]
        for field in range(fields):
            totals[field] = totals[field] + tile * full[field][:, start : start + lanes]
    for field in range(fields):
        out[field, :] = jnp.sum(totals[field].T, axis=0)


def on_device(band_pattern, density_in, field_terms, fit_blocks, tensor, metric_inv):
    count_rows = density_in.shape[0]
    blk = density_in.shape[-1]
    fields = field_terms.shape[0]
    slots = lax.axis_size("orb")
    half = slots // 2
    aux_count = lax.axis_size("aux")
    total_rows = count_rows * aux_count
    my_aux = lax.axis_index("aux")
    my_slot = lax.axis_index("orb")
    first_row = my_aux * count_rows
    side_a, side_b = half - 1, half
    is_a = my_slot < half
    middle = (my_slot == side_a) | (my_slot == side_b)
    zero_half = jnp.zeros((), jnp.bfloat16)
    up_rows, down_rows = 2 * half, 2 * half - 2
    forward = [(i, i + 1) for i in range(aux_count - 1)]
    backward = [(i + 1, i) for i in range(aux_count - 1)]
    cross = [(side_a, side_b), (side_b, side_a)]

    keep_rows = band_keep(band_pattern, first_row, total_rows)
    keep_own = lax.dynamic_index_in_dim(keep_rows, my_slot, 1, keepdims=False)
    density = jnp.where(keep_own[:, None, None], density_in[:, 0], zero_half)
    perturbed = jnp.where(keep_own[None, :, None, None], field_terms[:, :, 0], zero_half)

    inputs, moves = [], []

    def place(kind, field, distance, start, size, row):
        moves.append((kind, field, distance, len(inputs), start, size, row))

    def stage_rims(pieces, extra=None):
        low = [rows[count_rows - up_rows :] for _, _, _, rows in pieces]
        high = [rows[:down_rows] for _, _, _, rows in pieces]
        if extra is not None:
            low, high = low + [extra], high + [extra]
        low = lax.ppermute(jnp.concatenate(low, 0), "aux", forward)
        high = lax.ppermute(jnp.concatenate(high, 0), "aux", backward)
        for index, (kind, field, distance, _) in enumerate(pieces):
            place(kind, field, distance, index * up_rows, up_rows, 0)
        inputs.append(low)
        for index, (kind, field, distance, _) in enumerate(pieces):
            place(kind, field, distance, index * down_rows, down_rows, up_rows + count_rows)
        inputs.append(high)
        return low, high

    def whole(kind, distance, rows):
        if kind == "field":
            for field in range(fields):
                place(kind, field, distance, field * count_rows, count_rows, up_rows)
            inputs.append(rows.reshape((fields * count_rows,) + rows.shape[2:]))
        else:
            place(kind, 0, distance, 0, count_rows, up_rows)
            inputs.append(rows)

    inward = lambda d: [(side_a - d, side_a), (side_b + d, side_b)]
    side_density, side_fields, other_density = [density], [perturbed], []
    for distance in range(1, half):
        side_density.append(lax.ppermute(density, "orb", inward(distance)))
    other_density.append(lax.ppermute(density, "orb", cross))
    for distance in range(1, half):
        side_fields.append(lax.ppermute(perturbed, "orb", inward(distance)))

    pattern = jnp.pad(
        band_pattern.astype(jnp.bfloat16), ((0, blk - count_rows), (0, blk - slots))
    )[None]
    own = [("side", 0, 0, density)] + [("field", k, 0, perturbed[k]) for k in range(fields)]
    low, high = stage_rims(own, pattern)
    pattern_low = low[-1, count_rows - half : count_rows, :slots].astype(jnp.int32)
    pattern_high = high[-1, : half - 1, :slots].astype(jnp.int32)
    whole("side", 0, density)
    whole("field", 0, perturbed)

    for distance in range(1, half):
        other_density.append(lax.ppermute(side_density[distance], "orb", cross))
        stage_rims(
            [("side", 0, distance, side_density[distance]), ("other", 0, distance - 1, other_density[distance - 1])]
        )
        whole("side", distance, side_density[distance])
        whole("other", distance - 1, other_density[distance - 1])
    last = [("other", 0, half - 1, other_density[half - 1])]
    for distance in range(1, half):
        last += [("field", k, distance, side_fields[distance][k]) for k in range(fields)]
        whole("field", distance, side_fields[distance])
    whole("other", half - 1, other_density[half - 1])
    stage_rims(last)

    pattern_wide = jnp.concatenate([pattern_low, band_pattern, pattern_high], 0)
    keep_wide = band_keep(pattern_wide, first_row - half, total_rows).astype(jnp.int32)
    owner = fit_blocks[0] // count_rows == my_aux
    scal = jnp.stack(
        [middle.astype(jnp.int32), is_a.astype(jnp.int32), fit_blocks[0] % count_rows, owner.astype(jnp.int32)]
    )
    wide_rows = count_rows + up_rows + down_rows
    mid_rows = count_rows + 2 * half - 1
    plan = {"inputs": len(inputs), "moves": tuple(moves)}
    out_shape = [jax.ShapeDtypeStruct((fields, count_rows, blk, blk), jnp.bfloat16)] * slots
    out_shape += [jax.ShapeDtypeStruct((fields, blk, blk), jnp.bfloat16)] * slots
    results = pl.pallas_call(
        functools.partial(mid_kernel, slots, count_rows, fields, plan),
        out_shape=out_shape,
        in_specs=[SMEM, SMEM] + [ANY] * len(inputs),
        out_specs=[VMEM] * (2 * slots),
        scratch_shapes=[
            pltpu.VMEM((wide_rows, blk, slots * blk), jnp.bfloat16),
            pltpu.VMEM((fields, wide_rows, blk, half * blk), jnp.bfloat16),
            pltpu.VMEM((mid_rows, blk, slots * blk), jnp.bfloat16),
            pltpu.VMEM((fields, mid_rows, blk, slots * blk), jnp.bfloat16),
            pltpu.SemaphoreType.DMA((len(moves),)),
        ],
        name="mid_products",
    )(scal, keep_wide, *inputs)
    parts, fit_parts = results[:slots], results[slots:]

    def scatter(blocks, gate=None):
        got = []
        for step in range(1, slots):
            pairs = [(side_a, (side_a + step) % slots), (side_b, (side_b - step) % slots)]
            got.append(lax.ppermute(blocks[step], "orb", pairs))
        return got

    def add_up(first, others):
        total = first.astype(jnp.float32)
        for other in others:
            total = total + other.astype(jnp.float32)
        return total.astype(jnp.bfloat16)

    fit_own = add_up(fit_parts[0], scatter(fit_parts))
    response = add_up(parts[0], scatter(parts))[:, :, None]
    distance = 1
    while distance < aux_count:
        fit_own = fit_own + lax.ppermute(fit_own, "aux", swap_pairs(aux_count, distance))
        distance *= 2

    flat = fit_own.reshape(fields, -1)
    integrals = tensor.reshape(tensor.shape[1], -1)
    aux_rows, length = integrals.shape
    steps = 8
    sums = pl.pallas_call(
        sums_kernel,
        grid=(steps,),
        out_shape=jax.ShapeDtypeStruct((fields, aux_rows), jnp.float32),
        in_specs=[
            pl.BlockSpec((fields, length // steps), lambda i: (0, i)),
            pl.BlockSpec((aux_rows, length // steps), lambda i: (0, i)),
        ],
        out_specs=pl.BlockSpec((fields, aux_rows), lambda i: (0, 0)),
        scratch_shapes=[pltpu.VMEM((fields, aux_rows), jnp.float32)],
        name="fit_sums",
    )(flat, integrals)
    gathered = sums[None]
    distance = 1
    while distance < aux_count:
        got = lax.ppermute(gathered, "aux", swap_pairs(aux_count, distance))
        first = (my_aux & distance) == 0
        gathered = jnp.concatenate([jnp.where(first, gathered, got), jnp.where(first, got, gathered)], 0)
        distance *= 2
    coefficients = pl.pallas_call(
        metric_kernel,
        out_shape=jax.ShapeDtypeStruct((fields, metric_inv.shape[1]), jnp.float32),
        in_specs=[VMEM, VMEM],
        out_specs=VMEM,
        name="metric",
    )(gathered, metric_inv[0])
    distance = 1
    while distance < slots:
        coefficients = coefficients + lax.ppermute(coefficients, "orb", swap_pairs(slots, distance))
        distance *= 2
    return (response, coefficients[None])


def solution(mesh):
    in_specs = (
        P("aux", None),
        P("aux", "orb", None, None),
        P(None, "aux", "orb", None, None),
        P(),
        P(None, "aux", "orb", None),
        P(None, "aux", None),
    )
    out_specs = (P(None, "aux", "orb", None, None), P(None, None, "aux"))
    return jax.shard_map(
        on_device, mesh=mesh, in_specs=in_specs, out_specs=out_specs, check_vma=False
    )
```

```python
import functools

import jax
import jax.numpy as jnp
from jax import lax
from jax.experimental import pallas as pl
from jax.experimental.pallas import tpu as pltpu
from jax.sharding import PartitionSpec as P


ANY = pl.BlockSpec(memory_space=pl.ANY)
SMEM = pl.BlockSpec(memory_space=pltpu.SMEM)
VMEM = pl.BlockSpec(memory_space=pltpu.VMEM)


def band_keep(band_pattern, first_row, total_rows):
    slot_count = band_pattern.shape[1]
    half_band = slot_count // 2
    row_ids = first_row + jnp.arange(band_pattern.shape[0], dtype=jnp.int32)[:, None]
    columns = row_ids + jnp.arange(slot_count, dtype=jnp.int32)[None, :] - half_band
    return (band_pattern == 1) & (columns >= 0) & (columns < total_rows)


def swap_pairs(count, distance):
    return [(i, i ^ distance) for i in range(count)]


def mid_kernel(slots, count_rows, plan, scal, keep, *refs):
    half = slots // 2
    blk = refs[0].shape[-1]
    ins, rest = refs[: plan["inputs"]], refs[plan["inputs"] :]
    outs, rest = rest[:slots], rest[slots:]
    fits, rest = rest[:slots], rest[slots:]
    dens, pert, square, order, sems = rest
    mid_rows = count_rows + 2 * half - 1
    middle, is_a, fit_row, owner = scal[0], scal[1], scal[2], scal[3]

    def cols(slot, width=1):
        return pl.ds(slot * blk, width * blk)

    def wide(ref, row, low, high, head, tail):
        parts = [ref[row, :, cols(low, high - low)]]
        if head:
            parts.insert(0, jnp.zeros((blk, head * blk), jnp.bfloat16))
        if tail:
            parts.append(jnp.zeros((blk, tail * blk), jnp.bfloat16))
        return parts[0] if len(parts) == 1 else jnp.concatenate(parts, 1)

    def add_products(total, lefts, left_row, right, right_row):
        for first in range(0, slots, 2):
            rows, spans = [], []
            for t in (first, first + 1):
                low, high = max(0, t - half), min(slots - 1, slots - 1 + t - half)
                spans.append((t, low, high))
            start, stop = min(v[1] for v in spans), max(v[2] for v in spans)
            for t, low, high in spans:
                u = low - t + half
                rows.append(
                    wide(right, right_row + t, u, u + high - low + 1, low - start, stop - high)
                )
            lhs = [left[left_row, :, cols(first, 2)] for _, left in lefts]
            lhs = lhs[0] if len(lhs) == 1 else jnp.concatenate(lhs, 0)
            value = jnp.dot(lhs, jnp.concatenate(rows, 0), preferred_element_type=jnp.float32)
            for index, (key, _) in enumerate(lefts):
                for s in range(start, stop + 1):
                    part = value[index * blk : (index + 1) * blk, (s - start) * blk : (s - start + 1) * blk]
                    total[key, s] = total[key, s] + part if (key, s) in total else part

    def first_step(j, carry):
        total = {}
        add_products(total, [("square", dens), ("order", pert)], j + half, dens, j)
        add_products(total, [("order", dens)], j + half, pert, j)
        for s in range(slots):
            kept = keep[j, s] != 0
            square[j, :, cols(s)] = jnp.where(kept, total["square", s], 0.0).astype(jnp.bfloat16)
            order[j, :, cols(s)] = jnp.where(kept, total["order", s], 0.0).astype(jnp.bfloat16)
        return carry

    def second_step(i, carry):
        j = i + half
        total = {}
        add_products(total, [("second", square)], j, order, i)
        add_products(total, [("second", order)], j, square, i)
        for s in range(slots):
            twice = 2.0 * order[j, :, cols(s)].astype(jnp.float32)
            value = jnp.where(keep[j, s] != 0, twice - total["second", s], 0.0).astype(jnp.bfloat16)
            step = jnp.where(is_a != 0, (s - (half - 1)) % slots, (half - s) % slots)
            for place in range(slots):

                @pl.when(step == place)
                def _(place=place, value=value):
                    outs[place][i] = value

        return carry

    @pl.when(middle != 0)
    def _():
        copies = []
        for kind, field, distance, source, start, size, row in plan["moves"]:
            low, high = half - 1 - distance, half + distance
            slot = jnp.where((is_a != 0) == (kind == "near"), low, high)
            target = pert if field else dens
            copies.append(
                pltpu.make_async_copy(
                    ins[source].at[pl.ds(start, size)],
                    target.at[pl.ds(row, size), :, pl.ds(pl.multiple_of(slot * blk, blk), blk)],
                    sems.at[len(copies)],
                )
            )
        for copy in copies:
            copy.start()
        for copy in copies:
            copy.wait()
        lax.fori_loop(0, mid_rows, first_step, 0)
        lax.fori_loop(0, count_rows, second_step, 0)
        for step in range(slots):
            value = outs[step][fit_row].astype(jnp.float32)
            fits[step][...] = jnp.where(owner != 0, value, 0.0).astype(jnp.bfloat16)

    @pl.when(middle == 0)
    def _():
        outs[0][...] = jnp.zeros_like(outs[0])
        fits[0][...] = jnp.zeros_like(fits[0])


def sums_kernel(steps, place, *refs):
    pieces, rest = refs[:-4], refs[-4:]
    tensor, out, held, sems = rest
    fields, rows, blk = pieces[0].shape
    width = rows * blk // steps
    copies = [
        pltpu.make_async_copy(
            tensor.at[:, pl.ds(step * width, width)], held.at[:, pl.ds(step * width, width)], sems.at[step]
        )
        for step in range(steps)
    ]
    for copy in copies:
        copy.start()
    pairs = pieces[0][...]
    for piece in pieces[1:]:
        pairs = pairs + piece[...]
    out[...] = jnp.zeros_like(out)
    flat = pairs.reshape(fields, rows * blk)
    total = jnp.zeros((fields, held.shape[0]), jnp.float32)
    for step in range(steps):
        copies[step].wait()
        total = total + lax.dot_general(
            flat[:, step * width : (step + 1) * width],
            held[:, step * width : (step + 1) * width],
            (((1,), (1,)), ((), ())),
            preferred_element_type=jnp.float32,
        )
    out[place[0]] = total


def metric_kernel(steps, *refs):
    pieces, rest = refs[:-4], refs[-4:]
    metric, out, held, sems = rest
    width = metric.shape[1] // steps
    copies = [
        pltpu.make_async_copy(
            metric.at[:, pl.ds(step * width, width)], held.at[:, pl.ds(step * width, width)], sems.at[step]
        )
        for step in range(steps)
    ]
    for copy in copies:
        copy.start()
    sums = pieces[0][...]
    for piece in pieces[1:]:
        sums = sums + piece[...]
    groups, fields, wide = sums.shape
    rows, lanes = out.shape[1], 128
    totals = [jnp.zeros((rows, lanes), jnp.float32) for _ in range(fields)]
    full = [
        jnp.concatenate([sums[group, field : field + 1, :] for group in range(groups)], 1)
        for field in range(fields)
    ]
    for step in range(steps):
        copies[step].wait()
        for start in range(step * width, (step + 1) * width, lanes):
            tile = held[:, start : start + lanes]
            for field in range(fields):
                totals[field] = totals[field] + tile * full[field][:, start : start + lanes]
    for field in range(fields):
        out[field, :] = jnp.sum(totals[field].T, axis=0)


def on_device(band_pattern, density_in, field_terms, fit_blocks, tensor, metric_inv):
    count_rows = density_in.shape[0]
    blk = density_in.shape[-1]
    fields = field_terms.shape[0]
    slots = lax.axis_size("orb")
    half = slots // 2
    aux_count = lax.axis_size("aux")
    total_rows = count_rows * aux_count
    my_aux = lax.axis_index("aux")
    my_slot = lax.axis_index("orb")
    first_row = my_aux * count_rows
    side_a, side_b = half - 1, half
    is_a = my_slot < half
    middle = (my_slot == side_a) | (my_slot == side_b)
    zero_half = jnp.zeros((), jnp.bfloat16)
    up_rows, down_rows = 2 * half, 2 * half - 2
    forward = [(i, i + 1) for i in range(aux_count - 1)]
    backward = [(i + 1, i) for i in range(aux_count - 1)]

    keep_rows = band_keep(band_pattern, first_row, total_rows)
    keep_own = lax.dynamic_index_in_dim(keep_rows, my_slot, 1, keepdims=False)[:, None, None]
    density = jnp.where(keep_own, density_in[:, 0], zero_half)

    def with_field(index):
        picked = lax.dynamic_index_in_dim(field_terms, index, 0, keepdims=False)[:, 0]
        return jnp.concatenate([density, jnp.where(keep_own, picked, zero_half)], 0)

    near = with_field(jnp.where(is_a, 0, 1))
    far = with_field(jnp.where(is_a, 1, 0))

    inputs, moves = [], []

    def stage_rims(pieces, extra=None):
        split = lambda rows: (rows[:count_rows], rows[count_rows:])
        low = [part[count_rows - up_rows :] for _, _, rows in pieces for part in split(rows)]
        high = [part[:down_rows] for _, _, rows in pieces for part in split(rows)]
        if extra is not None:
            low, high = low + [extra], high + [extra]
        low = lax.ppermute(jnp.concatenate(low, 0), "aux", forward)
        high = lax.ppermute(jnp.concatenate(high, 0), "aux", backward)
        for source, size, row in ((low, up_rows, 0), (high, down_rows, up_rows + count_rows)):
            for index, (kind, distance, _) in enumerate(pieces):
                for field in range(2):
                    start = (2 * index + field) * size
                    moves.append((kind, field, distance, len(inputs), start, size, row))
            inputs.append(source)
        for kind, distance, rows in pieces:
            for field in range(2):
                moves.append((kind, field, distance, len(inputs), field * count_rows, count_rows, up_rows))
            inputs.append(rows)
        return low, high

    near_got, far_got = {0: near}, {}
    for distance in range(half):
        if distance:
            with jax.named_scope(f"near_{distance}"):
                near_got[distance] = lax.ppermute(
                    near, "orb", [(side_a - distance, side_a), (side_b + distance, side_b)]
                )
        with jax.named_scope(f"far_{distance}"):
            far_got[distance] = lax.ppermute(
                far, "orb", [(side_a - distance, side_b), (side_b + distance, side_a)]
            )
    pattern = jnp.pad(
        band_pattern.astype(jnp.bfloat16), ((0, blk - count_rows), (0, blk - slots))
    )[None]
    with jax.named_scope("rims_own"):
        low, high = stage_rims([("near", 0, near)], pattern)
    pattern_low = low[-1, count_rows - half : count_rows, :slots].astype(jnp.int32)
    pattern_high = high[-1, : half - 1, :slots].astype(jnp.int32)
    for distance in range(1, half):
        with jax.named_scope(f"rims_{distance}"):
            stage_rims(
                [("near", distance, near_got[distance]), ("far", distance - 1, far_got[distance - 1])]
            )
    with jax.named_scope("rims_last"):
        stage_rims([("far", half - 1, far_got[half - 1])])

    pattern_wide = jnp.concatenate([pattern_low, band_pattern, pattern_high], 0)
    keep_wide = band_keep(pattern_wide, first_row - half, total_rows).astype(jnp.int32)
    owner = fit_blocks[0] // count_rows == my_aux
    scal = jnp.stack(
        [middle.astype(jnp.int32), is_a.astype(jnp.int32), fit_blocks[0] % count_rows, owner.astype(jnp.int32)]
    )
    wide_rows = count_rows + up_rows + down_rows
    mid_rows = count_rows + 2 * half - 1
    plan = {"inputs": len(inputs), "moves": tuple(moves)}
    out_shape = [jax.ShapeDtypeStruct((count_rows, blk, blk), jnp.bfloat16)] * slots
    out_shape += [jax.ShapeDtypeStruct((blk, blk), jnp.bfloat16)] * slots
    results = pl.pallas_call(
        functools.partial(mid_kernel, slots, count_rows, plan),
        out_shape=out_shape,
        in_specs=[SMEM, SMEM] + [ANY] * len(inputs),
        out_specs=[VMEM] * (2 * slots),
        scratch_shapes=[
            pltpu.VMEM((wide_rows, blk, slots * blk), jnp.bfloat16),
            pltpu.VMEM((wide_rows, blk, slots * blk), jnp.bfloat16),
            pltpu.VMEM((mid_rows, blk, slots * blk), jnp.bfloat16),
            pltpu.VMEM((mid_rows, blk, slots * blk), jnp.bfloat16),
            pltpu.SemaphoreType.DMA((len(moves),)),
        ],
        name="mid_products",
    )(scal, keep_wide, *inputs)
    parts, fit_parts = results[:slots], results[slots:]

    def scatter(blocks):
        got = [blocks[0]]
        for step in range(1, slots):
            pairs = [(side_a, (side_a + step) % slots), (side_b, (side_b - step) % slots)]
            got.append(lax.ppermute(blocks[step], "orb", pairs))
        picked = []
        for wanted in ((my_slot - side_a) % slots, (side_b - my_slot) % slots):
            value = got[0]
            for step in range(1, slots):
                value = jnp.where(wanted == step, got[step], value)
            picked.append(value)
        return jnp.stack(picked, 0)

    with jax.named_scope("fit_scatter"):
        fit_own = scatter(fit_parts)
    with jax.named_scope("main_scatter"):
        response = scatter(parts)[:, :, None]
    with jax.named_scope("fit_core"):
        fit_own = fit_own + lax.ppermute(fit_own, "aux", swap_pairs(aux_count, 1))
    with jax.named_scope("fit_plane"):
        fit_pieces = [fit_own] + [
            lax.ppermute(fit_own, "aux", swap_pairs(aux_count, distance)) for distance in range(2, aux_count, 2)
        ]

    integrals = tensor.reshape(tensor.shape[1], -1)
    aux_rows, length = integrals.shape
    steps = 8
    sums = pl.pallas_call(
        functools.partial(sums_kernel, steps),
        out_shape=jax.ShapeDtypeStruct((aux_count, fields, aux_rows), jnp.float32),
        in_specs=[SMEM] + [VMEM] * len(fit_pieces) + [ANY],
        out_specs=VMEM,
        scratch_shapes=[pltpu.VMEM((aux_rows, length), jnp.bfloat16), pltpu.SemaphoreType.DMA((steps,))],
        name="fit_sums",
    )(my_aux.astype(jnp.int32)[None], *fit_pieces, integrals)
    with jax.named_scope("sums_core"):
        sums = sums + lax.ppermute(sums, "aux", swap_pairs(aux_count, 1))
    with jax.named_scope("sums_plane"):
        pieces = [sums] + [
            lax.ppermute(sums, "aux", swap_pairs(aux_count, distance)) for distance in range(2, aux_count, 2)
        ]
    metric = metric_inv[0]
    part = pl.pallas_call(
        functools.partial(metric_kernel, 4),
        out_shape=jax.ShapeDtypeStruct((fields, metric.shape[0]), jnp.float32),
        in_specs=[VMEM] * len(pieces) + [ANY],
        out_specs=VMEM,
        scratch_shapes=[pltpu.VMEM(metric.shape, jnp.float32), pltpu.SemaphoreType.DMA((4,))],
        name="metric",
    )(*pieces, metric)
    with jax.named_scope("last_sum"):
        got = [part] + [
            lax.ppermute(part, "orb", [(i, (i + step) % slots) for i in range(slots)]) for step in range(1, slots)
        ]
        coefficients = None
        for plane in range(slots):
            value = got[0]
            for step in range(1, slots):
                value = jnp.where((my_slot - plane) % slots == step, got[step], value)
            coefficients = value if coefficients is None else coefficients + value
    return (response, coefficients[None])


def solution(mesh):
    in_specs = (
        P("aux", None),
        P("aux", "orb", None, None),
        P(None, "aux", "orb", None, None),
        P(),
        P(None, "aux", "orb", None),
        P(None, "aux", None),
    )
    out_specs = (P(None, "aux", "orb", None, None), P(None, None, "aux"))
    return jax.shard_map(
        on_device, mesh=mesh, in_specs=in_specs, out_specs=out_specs, check_vma=False
    )
```

```python
import functools

import jax
import jax.numpy as jnp
from jax import lax
from jax.experimental import pallas as pl
from jax.experimental.pallas import tpu as pltpu
from jax.sharding import PartitionSpec as P


ANY = pl.BlockSpec(memory_space=pl.ANY)
SMEM = pl.BlockSpec(memory_space=pltpu.SMEM)
VMEM = pl.BlockSpec(memory_space=pltpu.VMEM)


def band_keep(band_pattern, first_row, total_rows):
    slot_count = band_pattern.shape[1]
    half_band = slot_count // 2
    row_ids = first_row + jnp.arange(band_pattern.shape[0], dtype=jnp.int32)[:, None]
    columns = row_ids + jnp.arange(slot_count, dtype=jnp.int32)[None, :] - half_band
    return (band_pattern == 1) & (columns >= 0) & (columns < total_rows)


def swap_pairs(count, distance):
    return [(i, i ^ distance) for i in range(count)]


def in_groups(count, group, step):
    group = min(group, count)
    trips = -(-count // group)
    if trips == 1:
        for place in range(count):
            step(place)
        return

    def body(trip, carry):
        start = jnp.minimum(trip * group, count - group)
        for place in range(group):
            step(start + place)
        return carry

    lax.fori_loop(0, trips, body, 0)


def mid_kernel(slots, count_rows, group, plan, scal, keep, *refs):
    half = slots // 2
    blk = refs[0].shape[-1]
    ins, rest = refs[: plan["inputs"]], refs[plan["inputs"] :]
    outs, fits, dens, pert, square, order, sems = rest
    mid_rows = count_rows + 2 * half - 1
    middle, is_a, fit_row, owner = scal[0], scal[1], scal[2], scal[3]

    def cols(slot, width=1):
        return pl.ds(slot * blk, width * blk)

    def wide(ref, row, low, high, head, tail):
        parts = [ref[row, :, cols(low, high - low)]]
        if head:
            parts.insert(0, jnp.zeros((blk, head * blk), jnp.bfloat16))
        if tail:
            parts.append(jnp.zeros((blk, tail * blk), jnp.bfloat16))
        return parts[0] if len(parts) == 1 else jnp.concatenate(parts, 1)

    def add_products(total, lefts, left_row, right, right_row):
        for first in range(0, slots, 2):
            rows, spans = [], []
            for t in (first, first + 1):
                low, high = max(0, t - half), min(slots - 1, slots - 1 + t - half)
                spans.append((t, low, high))
            start, stop = min(v[1] for v in spans), max(v[2] for v in spans)
            for t, low, high in spans:
                u = low - t + half
                rows.append(
                    wide(right, right_row + t, u, u + high - low + 1, low - start, stop - high)
                )
            lhs = [left[left_row, :, cols(first, 2)] for _, left in lefts]
            lhs = lhs[0] if len(lhs) == 1 else jnp.concatenate(lhs, 0)
            value = jnp.dot(lhs, jnp.concatenate(rows, 0), preferred_element_type=jnp.float32)
            for index, (key, _) in enumerate(lefts):
                for s in range(start, stop + 1):
                    part = value[index * blk : (index + 1) * blk, (s - start) * blk : (s - start + 1) * blk]
                    total[key, s] = total[key, s] + part if (key, s) in total else part

    def first_step(j):
        total = {}
        add_products(total, [("square", dens), ("order", pert)], j + half, dens, j)
        add_products(total, [("order", dens)], j + half, pert, j)
        for s in range(slots):
            kept = keep[j, s] != 0
            square[j, :, cols(s)] = jnp.where(kept, total["square", s], 0.0).astype(jnp.bfloat16)
            order[j, :, cols(s)] = jnp.where(kept, total["order", s], 0.0).astype(jnp.bfloat16)

    def second_step(i):
        j = i + half
        total = {}
        add_products(total, [("second", square)], j, order, i)
        add_products(total, [("second", order)], j, square, i)
        for s in range(slots):
            twice = 2.0 * order[j, :, cols(s)].astype(jnp.float32)
            value = jnp.where(keep[j, s] != 0, twice - total["second", s], 0.0).astype(jnp.bfloat16)
            outs[jnp.where(is_a != 0, (s - (half - 1)) % slots, (half - s) % slots), i] = value

    @pl.when(middle != 0)
    def _():
        copies = []
        for kind, field, distance, source, start, size, row in plan["moves"]:
            low, high = half - 1 - distance, half + distance
            slot = jnp.where((is_a != 0) == (kind == "near"), low, high)
            target = pert if field else dens
            copies.append(
                pltpu.make_async_copy(
                    ins[source].at[pl.ds(start, size)],
                    target.at[pl.ds(row, size), :, pl.ds(pl.multiple_of(slot * blk, blk), blk)],
                    sems.at[len(copies)],
                )
            )
        for copy in copies:
            copy.start()
        for copy in copies:
            copy.wait()
        in_groups(mid_rows, group, first_step)
        in_groups(count_rows, group, second_step)
        for step in range(slots):
            value = outs[step, fit_row].astype(jnp.float32)
            fits[step] = jnp.where(owner != 0, value, 0.0).astype(jnp.bfloat16)

    @pl.when(middle == 0)
    def _():
        outs[...] = jnp.zeros_like(outs)
        fits[...] = jnp.zeros_like(fits)


def preload_kernel(steps, *refs):
    count = len(refs) // 2
    sources, targets, sems = refs[:count], refs[count : 2 * count], refs[2 * count]
    copies = []
    for source, target in zip(sources, targets):
        height = source.shape[0] // steps
        for step in range(steps):
            rows = pl.ds(step * height, height)
            copies.append(pltpu.make_async_copy(source.at[rows], target.at[rows], sems.at[len(copies)]))
    for copy in copies:
        copy.start()
    for copy in copies:
        copy.wait()


def sums_kernel(place, *refs):
    pieces, (tensor, out) = refs[:-2], refs[-2:]
    pairs = pieces[0][...]
    for piece in pieces[1:]:
        pairs = pairs + piece[...]
    out[...] = jnp.zeros_like(out)
    flat = pairs.reshape(pairs.shape[0], -1)
    out[place[0]] = lax.dot_general(
        flat, tensor[...], (((1,), (1,)), ((), ())), preferred_element_type=jnp.float32
    )


def metric_kernel(*refs):
    pieces, (metric, out) = refs[:-2], refs[-2:]
    sums = pieces[0][...]
    for piece in pieces[1:]:
        sums = sums + piece[...]
    groups, fields, width = sums.shape
    lanes = 128
    totals = [jnp.zeros((out.shape[1], lanes), jnp.float32) for _ in range(fields)]
    full = [
        jnp.concatenate([sums[group, field : field + 1, :] for group in range(groups)], 1)
        for field in range(fields)
    ]
    for start in range(0, groups * width, lanes):
        tile = metric[:, start : start + lanes]
        for field in range(fields):
            totals[field] = totals[field] + tile * full[field][:, start : start + lanes]
    for field in range(fields):
        out[field, :] = jnp.sum(totals[field].T, axis=0)


def on_device(band_pattern, density_in, field_terms, fit_blocks, tensor, metric_inv):
    count_rows = density_in.shape[0]
    blk = density_in.shape[-1]
    fields = field_terms.shape[0]
    slots = lax.axis_size("orb")
    half = slots // 2
    aux_count = lax.axis_size("aux")
    total_rows = count_rows * aux_count
    my_aux = lax.axis_index("aux")
    my_slot = lax.axis_index("orb")
    first_row = my_aux * count_rows
    side_a, side_b = half - 1, half
    is_a = my_slot < half
    middle = (my_slot == side_a) | (my_slot == side_b)
    zero_half = jnp.zeros((), jnp.bfloat16)
    up_rows, down_rows = 2 * half, 2 * half - 2
    forward = [(i, i + 1) for i in range(aux_count - 1)]
    backward = [(i + 1, i) for i in range(aux_count - 1)]

    keep_rows = band_keep(band_pattern, first_row, total_rows)
    keep_own = lax.dynamic_index_in_dim(keep_rows, my_slot, 1, keepdims=False)[:, None, None]
    density = jnp.where(keep_own, density_in[:, 0], zero_half)

    def with_field(index):
        picked = lax.dynamic_index_in_dim(field_terms, index, 0, keepdims=False)[:, 0]
        return jnp.concatenate([density, jnp.where(keep_own, picked, zero_half)], 0)

    near = with_field(jnp.where(is_a, 0, 1))
    far = with_field(jnp.where(is_a, 1, 0))

    inputs, moves = [], []

    def stage_rims(pieces, extra=None):
        split = lambda rows: (rows[:count_rows], rows[count_rows:])
        low = [part[count_rows - up_rows :] for _, _, rows in pieces for part in split(rows)]
        high = [part[:down_rows] for _, _, rows in pieces for part in split(rows)]
        if extra is not None:
            low, high = low + [extra], high + [extra]
        low = lax.ppermute(jnp.concatenate(low, 0), "aux", forward)
        high = lax.ppermute(jnp.concatenate(high, 0), "aux", backward)
        for source, size, row in ((low, up_rows, 0), (high, down_rows, up_rows + count_rows)):
            for index, (kind, distance, _) in enumerate(pieces):
                for field in range(2):
                    start = (2 * index + field) * size
                    moves.append((kind, field, distance, len(inputs), start, size, row))
            inputs.append(source)
        for kind, distance, rows in pieces:
            for field in range(2):
                moves.append((kind, field, distance, len(inputs), field * count_rows, count_rows, up_rows))
            inputs.append(rows)
        return low, high

    near_got, far_got = {0: near}, {}
    for distance in range(half):
        if distance:
            near_got[distance] = lax.ppermute(near, "orb", [(side_a - distance, side_a), (side_b + distance, side_b)])
        far_got[distance] = lax.ppermute(
            far, "orb", [(side_a - distance, side_b), (side_b + distance, side_a)]
        )
    pattern = jnp.pad(
        band_pattern.astype(jnp.bfloat16), ((0, blk - count_rows), (0, blk - slots))
    )[None]
    low, high = stage_rims([("near", 0, near)], pattern)
    held = (tensor.reshape(tensor.shape[1], -1), metric_inv[0])
    steps = max(count for count in (1, 2, 4, 8) if held[0].shape[0] % (16 * count) == 0)
    held = pl.pallas_call(
        functools.partial(preload_kernel, steps),
        out_shape=[jax.ShapeDtypeStruct(value.shape, value.dtype) for value in held],
        in_specs=[pl.BlockSpec(memory_space=pltpu.HBM)] * 2,
        out_specs=[VMEM] * 2,
        scratch_shapes=[pltpu.SemaphoreType.DMA((2 * steps,))],
        compiler_params=pltpu.CompilerParams(vmem_limit_bytes=4 << 20),
        name="preload",
    )(*held)
    integrals, metric = (pltpu.with_memory_space_constraint(value, pltpu.VMEM) for value in held)
    pattern_low = low[-1, count_rows - half : count_rows, :slots].astype(jnp.int32)
    pattern_high = high[-1, : half - 1, :slots].astype(jnp.int32)
    for distance in range(1, half):
        stage_rims(
            [("near", distance, near_got[distance]), ("far", distance - 1, far_got[distance - 1])]
        )
    stage_rims([("far", half - 1, far_got[half - 1])])

    pattern_wide = jnp.concatenate([pattern_low, band_pattern, pattern_high], 0)
    keep_wide = band_keep(pattern_wide, first_row - half, total_rows).astype(jnp.int32)
    owner = fit_blocks[0] // count_rows == my_aux
    scal = jnp.stack(
        [middle.astype(jnp.int32), is_a.astype(jnp.int32), fit_blocks[0] % count_rows, owner.astype(jnp.int32)]
    )
    wide_rows = count_rows + up_rows + down_rows
    mid_rows = count_rows + 2 * half - 1
    plan = {"inputs": len(inputs), "moves": tuple(moves)}
    out_shape = [
        jax.ShapeDtypeStruct((slots, count_rows, blk, blk), jnp.bfloat16),
        jax.ShapeDtypeStruct((slots, blk, blk), jnp.bfloat16),
    ]
    blocks = 2 * (wide_rows + mid_rows) * slots + 2 * slots * (count_rows + 1)
    parts, fit_parts = pl.pallas_call(
        functools.partial(mid_kernel, slots, count_rows, 4 if slots <= 4 else 1, plan),
        out_shape=out_shape,
        in_specs=[SMEM, SMEM] + [ANY] * len(inputs),
        out_specs=[VMEM] * 2,
        scratch_shapes=[
            pltpu.VMEM((wide_rows, blk, slots * blk), jnp.bfloat16),
            pltpu.VMEM((wide_rows, blk, slots * blk), jnp.bfloat16),
            pltpu.VMEM((mid_rows, blk, slots * blk), jnp.bfloat16),
            pltpu.VMEM((mid_rows, blk, slots * blk), jnp.bfloat16),
            pltpu.SemaphoreType.DMA((len(moves),)),
        ],
        compiler_params=pltpu.CompilerParams(vmem_limit_bytes=blocks * blk * blk * 2 + (4 << 20)),
        name="mid_products",
    )(scal, keep_wide, *inputs)

    def scatter(blocks):
        got = [blocks[0]]
        for step in range(1, slots):
            pairs = [(side_a, (side_a + step) % slots), (side_b, (side_b - step) % slots)]
            got.append(lax.ppermute(blocks[step], "orb", pairs))
        picked = []
        for wanted in ((my_slot - side_a) % slots, (side_b - my_slot) % slots):
            value = got[0]
            for step in range(1, slots):
                value = jnp.where(wanted == step, got[step], value)
            picked.append(value)
        return jnp.stack(picked, 0)

    fit_own = scatter(fit_parts)
    response = scatter(parts)[:, :, None]
    fit_own = fit_own + lax.ppermute(fit_own, "aux", swap_pairs(aux_count, 1))
    fit_pieces = [fit_own] + [
        lax.ppermute(fit_own, "aux", swap_pairs(aux_count, distance)) for distance in range(2, aux_count, 2)
    ]

    aux_rows = integrals.shape[0]
    sums = pl.pallas_call(
        sums_kernel,
        out_shape=jax.ShapeDtypeStruct((aux_count, fields, aux_rows), jnp.float32),
        in_specs=[SMEM] + [VMEM] * (len(fit_pieces) + 1),
        out_specs=VMEM,
        compiler_params=pltpu.CompilerParams(vmem_limit_bytes=8 << 20),
        name="fit_sums",
    )(my_aux.astype(jnp.int32)[None], *fit_pieces, integrals)
    sums = sums + lax.ppermute(sums, "aux", swap_pairs(aux_count, 1))
    pieces = [sums] + [
        lax.ppermute(sums, "aux", swap_pairs(aux_count, distance)) for distance in range(2, aux_count, 2)
    ]
    part = pl.pallas_call(
        metric_kernel,
        out_shape=jax.ShapeDtypeStruct((fields, metric.shape[0]), jnp.float32),
        in_specs=[VMEM] * (len(pieces) + 1),
        out_specs=VMEM,
        compiler_params=pltpu.CompilerParams(vmem_limit_bytes=8 << 20),
        name="metric",
    )(*pieces, metric)
    got = [part] + [
        lax.ppermute(part, "orb", [(i, (i + step) % slots) for i in range(slots)]) for step in range(1, slots)
    ]
    coefficients = None
    for plane in range(slots):
        value = got[0]
        for step in range(1, slots):
            value = jnp.where((my_slot - plane) % slots == step, got[step], value)
        coefficients = value if coefficients is None else coefficients + value
    return (response, coefficients[None])


def solution(mesh):
    in_specs = (
        P("aux", None),
        P("aux", "orb", None, None),
        P(None, "aux", "orb", None, None),
        P(),
        P(None, "aux", "orb", None),
        P(None, "aux", None),
    )
    out_specs = (P(None, "aux", "orb", None, None), P(None, None, "aux"))

    return jax.shard_map(on_device, mesh=mesh, in_specs=in_specs, out_specs=out_specs, check_vma=False)
```

```python
import functools

import jax
import jax.numpy as jnp
from jax import lax
from jax.experimental import pallas as pl
from jax.experimental.pallas import tpu as pltpu
from jax.sharding import PartitionSpec as P


ANY = pl.BlockSpec(memory_space=pl.ANY)
SMEM = pl.BlockSpec(memory_space=pltpu.SMEM)
VMEM = pl.BlockSpec(memory_space=pltpu.VMEM)


def band_keep(band_pattern, first_row, total_rows):
    slot_count = band_pattern.shape[1]
    half_band = slot_count // 2
    row_ids = first_row + jnp.arange(band_pattern.shape[0], dtype=jnp.int32)[:, None]
    columns = row_ids + jnp.arange(slot_count, dtype=jnp.int32)[None, :] - half_band
    return (band_pattern == 1) & (columns >= 0) & (columns < total_rows)


def swap_pairs(count, distance):
    return [(i, i ^ distance) for i in range(count)]


def in_groups(count, group, step):
    group = min(group, count)
    trips = -(-count // group)
    if trips == 1:
        for place in range(count):
            step(place)
        return

    def body(trip, carry):
        start = jnp.minimum(trip * group, count - group)
        for place in range(group):
            step(start + place)
        return carry

    lax.fori_loop(0, trips, body, 0)


def mid_kernel(slots, count_rows, group, plan, scal, keep, *refs):
    half = slots // 2
    blk = refs[0].shape[-1]
    ins, rest = refs[: plan["inputs"]], refs[plan["inputs"] :]
    outs, fits, dens, pert, square, order, sems = rest
    mid_rows = count_rows + 2 * half - 1
    middle, is_a, fit_row, owner = scal[0], scal[1], scal[2], scal[3]

    def cols(slot, width=1):
        return pl.ds(slot * blk, width * blk)

    def wide(ref, row, low, high, head, tail):
        parts = [ref[row, :, cols(low, high - low)]]
        if head:
            parts.insert(0, jnp.zeros((blk, head * blk), jnp.bfloat16))
        if tail:
            parts.append(jnp.zeros((blk, tail * blk), jnp.bfloat16))
        return parts[0] if len(parts) == 1 else jnp.concatenate(parts, 1)

    def add_products(total, lefts, left_row, right, right_row):
        for first in range(0, slots, 2):
            rows, spans = [], []
            for t in (first, first + 1):
                low, high = max(0, t - half), min(slots - 1, slots - 1 + t - half)
                spans.append((t, low, high))
            start, stop = min(v[1] for v in spans), max(v[2] for v in spans)
            for t, low, high in spans:
                u = low - t + half
                rows.append(
                    wide(right, right_row + t, u, u + high - low + 1, low - start, stop - high)
                )
            lhs = [left[left_row, :, cols(first, 2)] for _, left in lefts]
            lhs = lhs[0] if len(lhs) == 1 else jnp.concatenate(lhs, 0)
            value = jnp.dot(lhs, jnp.concatenate(rows, 0), preferred_element_type=jnp.float32)
            for index, (key, _) in enumerate(lefts):
                for s in range(start, stop + 1):
                    part = value[index * blk : (index + 1) * blk, (s - start) * blk : (s - start + 1) * blk]
                    total[key, s] = total[key, s] + part if (key, s) in total else part

    def first_step(j):
        total = {}
        add_products(total, [("square", dens), ("order", pert)], j + half, dens, j)
        add_products(total, [("order", dens)], j + half, pert, j)
        for s in range(slots):
            kept = keep[j, s] != 0
            square[j, :, cols(s)] = jnp.where(kept, total["square", s], 0.0).astype(jnp.bfloat16)
            order[j, :, cols(s)] = jnp.where(kept, total["order", s], 0.0).astype(jnp.bfloat16)

    def second_step(i):
        j = i + half
        total = {}
        add_products(total, [("second", square)], j, order, i)
        add_products(total, [("second", order)], j, square, i)
        for s in range(slots):
            twice = 2.0 * order[j, :, cols(s)].astype(jnp.float32)
            value = jnp.where(keep[j, s] != 0, twice - total["second", s], 0.0).astype(jnp.bfloat16)
            outs[jnp.where(is_a != 0, (s - (half - 1)) % slots, (half - s) % slots), i] = value

    @pl.when(middle != 0)
    def _():
        copies = []
        for kind, field, distance, source, start, size, row in plan["moves"]:
            low, high = half - 1 - distance, half + distance
            slot = jnp.where((is_a != 0) == (kind == "near"), low, high)
            target = pert if field else dens
            copies.append(
                pltpu.make_async_copy(
                    ins[source].at[pl.ds(start, size)],
                    target.at[pl.ds(row, size), :, pl.ds(pl.multiple_of(slot * blk, blk), blk)],
                    sems.at[len(copies)],
                )
            )
        for copy in copies:
            copy.start()
        for copy in copies:
            copy.wait()
        in_groups(mid_rows, group, first_step)
        in_groups(count_rows, group, second_step)
        for step in range(slots):
            value = outs[step, fit_row].astype(jnp.float32)
            fits[step] = jnp.where(owner != 0, value, 0.0).astype(jnp.bfloat16)

    @pl.when(middle == 0)
    def _():
        outs[...] = jnp.zeros_like(outs)
        fits[...] = jnp.zeros_like(fits)


def preload_kernel(steps, *refs):
    count = len(refs) // 2
    sources, targets, sems = refs[:count], refs[count : 2 * count], refs[2 * count]
    copies = []
    for source, target in zip(sources, targets):
        height = source.shape[0] // steps
        for step in range(steps):
            rows = pl.ds(step * height, height)
            copies.append(pltpu.make_async_copy(source.at[rows], target.at[rows], sems.at[len(copies)]))
    for copy in copies:
        copy.start()
    for copy in copies:
        copy.wait()


def sums_kernel(place, *refs):
    pieces, (tensor, out) = refs[:-2], refs[-2:]
    pairs = pieces[0][...]
    for piece in pieces[1:]:
        pairs = pairs + piece[...]
    out[...] = jnp.zeros_like(out)
    flat = pairs.reshape(pairs.shape[0], -1)
    out[place[0]] = lax.dot_general(
        flat, tensor[...], (((1,), (1,)), ((), ())), preferred_element_type=jnp.float32
    )


def metric_kernel(*refs):
    pieces, (metric, out) = refs[:-2], refs[-2:]
    sums = pieces[0][...]
    for piece in pieces[1:]:
        sums = sums + piece[...]
    groups, fields, width = sums.shape
    lanes = 128
    totals = [jnp.zeros((out.shape[1], lanes), jnp.float32) for _ in range(fields)]
    full = [
        jnp.concatenate([sums[group, field : field + 1, :] for group in range(groups)], 1)
        for field in range(fields)
    ]
    for start in range(0, groups * width, lanes):
        tile = metric[:, start : start + lanes]
        for field in range(fields):
            totals[field] = totals[field] + tile * full[field][:, start : start + lanes]
    for field in range(fields):
        out[field, :] = jnp.sum(totals[field].T, axis=0)


def on_device(band_pattern, density_in, field_terms, fit_blocks, tensor, metric_inv):
    count_rows = density_in.shape[0]
    blk = density_in.shape[-1]
    fields = field_terms.shape[0]
    slots = lax.axis_size("orb")
    half = slots // 2
    aux_count = lax.axis_size("aux")
    total_rows = count_rows * aux_count
    my_aux = lax.axis_index("aux")
    my_slot = lax.axis_index("orb")
    first_row = my_aux * count_rows
    side_a, side_b = half - 1, half
    is_a = my_slot < half
    middle = (my_slot == side_a) | (my_slot == side_b)
    zero_half = jnp.zeros((), jnp.bfloat16)
    up_rows, down_rows = 2 * half, 2 * half - 2
    forward = [(i, i + 1) for i in range(aux_count - 1)]
    backward = [(i + 1, i) for i in range(aux_count - 1)]

    keep_rows = band_keep(band_pattern, first_row, total_rows)
    keep_own = lax.dynamic_index_in_dim(keep_rows, my_slot, 1, keepdims=False)[:, None, None]
    density = jnp.where(keep_own, density_in[:, 0], zero_half)

    def with_field(index):
        picked = lax.dynamic_index_in_dim(field_terms, index, 0, keepdims=False)[:, 0]
        return jnp.concatenate([density, jnp.where(keep_own, picked, zero_half)], 0)

    near = with_field(jnp.where(is_a, 0, 1))
    far = with_field(jnp.where(is_a, 1, 0))

    inputs, moves = [], []

    def stage_rims(pieces, extra=None):
        split = lambda rows: (rows[:count_rows], rows[count_rows:])
        low = [part[count_rows - up_rows :] for _, _, rows in pieces for part in split(rows)]
        high = [part[:down_rows] for _, _, rows in pieces for part in split(rows)]
        if extra is not None:
            low, high = low + [extra], high + [extra]
        low = lax.ppermute(jnp.concatenate(low, 0), "aux", forward)
        high = lax.ppermute(jnp.concatenate(high, 0), "aux", backward)
        for source, size, row in ((low, up_rows, 0), (high, down_rows, up_rows + count_rows)):
            for index, (kind, distance, _) in enumerate(pieces):
                for field in range(2):
                    start = (2 * index + field) * size
                    moves.append((kind, field, distance, len(inputs), start, size, row))
            inputs.append(source)
        for kind, distance, rows in pieces:
            for field in range(2):
                moves.append((kind, field, distance, len(inputs), field * count_rows, count_rows, up_rows))
            inputs.append(rows)
        return low, high

    wanted = [(my_slot - side_a) % slots, (side_b - my_slot) % slots]
    wanted += [(my_slot - plane) % slots for plane in range(slots)]
    wanted = [[index == step for step in range(slots)] for index in wanted]

    near_got, far_got = {0: near}, {}
    for distance in range(half):
        if distance:
            near_got[distance] = lax.ppermute(near, "orb", [(side_a - distance, side_a), (side_b + distance, side_b)])
        far_got[distance] = lax.ppermute(
            far, "orb", [(side_a - distance, side_b), (side_b + distance, side_a)]
        )
    pattern = jnp.pad(
        band_pattern.astype(jnp.bfloat16), ((0, blk - count_rows), (0, blk - slots))
    )[None]
    low, high = stage_rims([("near", 0, near)], pattern)
    source, metric_source, *flags = lax.optimization_barrier(
        [tensor, metric_inv] + [flag for group in wanted for flag in group]
    )
    wanted = [flags[index : index + slots] for index in range(0, len(flags), slots)]
    held = (source.reshape(tensor.shape[1], -1), metric_source[0])
    held = tuple(pltpu.with_memory_space_constraint(value, pltpu.HBM) for value in held)
    steps = max(count for count in (1, 2, 4, 8) if held[0].shape[0] % (16 * count) == 0)
    held = pl.pallas_call(
        functools.partial(preload_kernel, steps),
        out_shape=[jax.ShapeDtypeStruct(value.shape, value.dtype) for value in held],
        in_specs=[pl.BlockSpec(memory_space=pltpu.HBM)] * 2,
        out_specs=[VMEM] * 2,
        scratch_shapes=[pltpu.SemaphoreType.DMA((2 * steps,))],
        compiler_params=pltpu.CompilerParams(vmem_limit_bytes=4 << 20),
        name="preload",
    )(*held)
    integrals, metric = (pltpu.with_memory_space_constraint(value, pltpu.VMEM) for value in held)
    pattern_low = low[-1, count_rows - half : count_rows, :slots].astype(jnp.int32)
    pattern_high = high[-1, : half - 1, :slots].astype(jnp.int32)
    for distance in range(1, half):
        stage_rims(
            [("near", distance, near_got[distance]), ("far", distance - 1, far_got[distance - 1])]
        )
    stage_rims([("far", half - 1, far_got[half - 1])])

    pattern_wide = jnp.concatenate([pattern_low, band_pattern, pattern_high], 0)
    keep_wide = band_keep(pattern_wide, first_row - half, total_rows).astype(jnp.int32)
    owner = fit_blocks[0] // count_rows == my_aux
    scal = jnp.stack(
        [middle.astype(jnp.int32), is_a.astype(jnp.int32), fit_blocks[0] % count_rows, owner.astype(jnp.int32)]
    )
    wide_rows = count_rows + up_rows + down_rows
    mid_rows = count_rows + 2 * half - 1
    plan = {"inputs": len(inputs), "moves": tuple(moves)}
    out_shape = [
        jax.ShapeDtypeStruct((slots, count_rows, blk, blk), jnp.bfloat16),
        jax.ShapeDtypeStruct((slots, blk, blk), jnp.bfloat16),
    ]
    blocks = 2 * (wide_rows + mid_rows) * slots + 2 * slots * (count_rows + 1)
    parts, fit_parts = pl.pallas_call(
        functools.partial(mid_kernel, slots, count_rows, 4 if slots <= 4 else 1, plan),
        out_shape=out_shape,
        in_specs=[SMEM, SMEM] + [ANY] * len(inputs),
        out_specs=[VMEM] * 2,
        scratch_shapes=[
            pltpu.VMEM((wide_rows, blk, slots * blk), jnp.bfloat16),
            pltpu.VMEM((wide_rows, blk, slots * blk), jnp.bfloat16),
            pltpu.VMEM((mid_rows, blk, slots * blk), jnp.bfloat16),
            pltpu.VMEM((mid_rows, blk, slots * blk), jnp.bfloat16),
            pltpu.SemaphoreType.DMA((len(moves),)),
        ],
        compiler_params=pltpu.CompilerParams(vmem_limit_bytes=blocks * blk * blk * 2 + (4 << 20)),
        name="mid_products",
    )(scal, keep_wide, *inputs)

    def scatter(blocks):
        got = [blocks[0]]
        for step in range(1, slots):
            pairs = [(side_a, (side_a + step) % slots), (side_b, (side_b - step) % slots)]
            got.append(lax.ppermute(blocks[step], "orb", pairs))
        return got

    def assemble(got):
        picked = []
        for flags in wanted[:fields]:
            value = got[0]
            for step in range(1, slots):
                value = jnp.where(flags[step], got[step], value)
            picked.append(value)
        return jnp.stack(picked, 0)

    fit_own = assemble(scatter(fit_parts))
    got = scatter(parts)
    response = assemble(got)[:, :, None]
    fit_own = fit_own + lax.ppermute(fit_own, "aux", swap_pairs(aux_count, 1))
    fit_pieces = [fit_own] + [
        lax.ppermute(fit_own, "aux", swap_pairs(aux_count, distance)) for distance in range(2, aux_count, 2)
    ]

    aux_rows = integrals.shape[0]
    sums = pl.pallas_call(
        sums_kernel,
        out_shape=jax.ShapeDtypeStruct((aux_count, fields, aux_rows), jnp.float32),
        in_specs=[SMEM] + [VMEM] * (len(fit_pieces) + 1),
        out_specs=VMEM,
        compiler_params=pltpu.CompilerParams(vmem_limit_bytes=8 << 20),
        name="fit_sums",
    )(my_aux.astype(jnp.int32)[None], *fit_pieces, integrals)
    sums = sums + lax.ppermute(sums, "aux", swap_pairs(aux_count, 1))
    pieces = [sums] + [
        lax.ppermute(sums, "aux", swap_pairs(aux_count, distance)) for distance in range(2, aux_count, 2)
    ]
    part = pl.pallas_call(
        metric_kernel,
        out_shape=jax.ShapeDtypeStruct((fields, metric.shape[0]), jnp.float32),
        in_specs=[VMEM] * (len(pieces) + 1),
        out_specs=VMEM,
        compiler_params=pltpu.CompilerParams(vmem_limit_bytes=8 << 20),
        name="metric",
    )(*pieces, metric)
    got = [part] + [
        lax.ppermute(part, "orb", [(i, (i + step) % slots) for i in range(slots)]) for step in range(1, slots)
    ]
    coefficients = None
    for plane in range(slots):
        value = got[0]
        for step in range(1, slots):
            value = jnp.where(wanted[fields + plane][step], got[step], value)
        coefficients = value if coefficients is None else coefficients + value
    return (response, coefficients[None])


def solution(mesh):
    in_specs = (
        P("aux", None),
        P("aux", "orb", None, None),
        P(None, "aux", "orb", None, None),
        P(),
        P(None, "aux", "orb", None),
        P(None, "aux", None),
    )
    out_specs = (P(None, "aux", "orb", None, None), P(None, None, "aux"))

    return jax.shard_map(on_device, mesh=mesh, in_specs=in_specs, out_specs=out_specs, check_vma=False)
```

```python
import functools

import jax
import jax.numpy as jnp
from jax import lax
from jax.experimental import pallas as pl
from jax.experimental.pallas import tpu as pltpu
from jax.sharding import PartitionSpec as P


ANY = pl.BlockSpec(memory_space=pl.ANY)
SMEM = pl.BlockSpec(memory_space=pltpu.SMEM)
VMEM = pl.BlockSpec(memory_space=pltpu.VMEM)


def band_keep(band_pattern, first_row, total_rows):
    slot_count = band_pattern.shape[1]
    half_band = slot_count // 2
    row_ids = first_row + jnp.arange(band_pattern.shape[0], dtype=jnp.int32)[:, None]
    columns = row_ids + jnp.arange(slot_count, dtype=jnp.int32)[None, :] - half_band
    return (band_pattern == 1) & (columns >= 0) & (columns < total_rows)


def swap_pairs(count, distance):
    return [(i, i ^ distance) for i in range(count)]


def in_groups(count, group, step):
    group = min(group, count)
    trips = -(-count // group)
    if trips == 1:
        for place in range(count):
            step(place)
        return

    def body(trip, carry):
        start = jnp.minimum(trip * group, count - group)
        for place in range(group):
            step(start + place)
        return carry

    lax.fori_loop(0, trips, body, 0)


def cols(slot, width, blk):
    return pl.ds(slot * blk, width * blk)


def wide(ref, row, low, high, head, tail):
    blk = ref.shape[1]
    parts = [ref[row, :, cols(low, high - low, blk)]]
    if head:
        parts.insert(0, jnp.zeros((blk, head * blk), jnp.bfloat16))
    if tail:
        parts.append(jnp.zeros((blk, tail * blk), jnp.bfloat16))
    return parts[0] if len(parts) == 1 else jnp.concatenate(parts, 1)


def add_products(slots, total, lefts, left_row, right, right_row):
    half, blk = slots // 2, right.shape[1]
    for first in range(0, slots, 2):
        rows, spans = [], []
        for t in (first, first + 1):
            low, high = max(0, t - half), min(slots - 1, slots - 1 + t - half)
            spans.append((t, low, high))
        start, stop = min(v[1] for v in spans), max(v[2] for v in spans)
        for t, low, high in spans:
            u = low - t + half
            rows.append(
                wide(right, right_row + t, u, u + high - low + 1, low - start, stop - high)
            )
        lhs = [left[left_row, :, cols(first, 2, blk)] for _, left in lefts]
        lhs = lhs[0] if len(lhs) == 1 else jnp.concatenate(lhs, 0)
        value = jnp.dot(lhs, jnp.concatenate(rows, 0), preferred_element_type=jnp.float32)
        for index, (key, _) in enumerate(lefts):
            for s in range(start, stop + 1):
                part = value[index * blk : (index + 1) * blk, (s - start) * blk : (s - start + 1) * blk]
                total[key, s] = total[key, s] + part if (key, s) in total else part


def response_row(slots, keep, square, order, i, write):
    half, blk = slots // 2, square.shape[1]
    j = i + half
    total = {}
    add_products(slots, total, [("second", square)], j, order, i)
    add_products(slots, total, [("second", order)], j, square, i)
    for s in range(slots):
        twice = 2.0 * order[j, :, cols(s, 1, blk)].astype(jnp.float32)
        write(s, jnp.where(keep[j, s] != 0, twice - total["second", s], 0.0).astype(jnp.bfloat16))


def place_of(slots, is_a, slot):
    half = slots // 2
    return jnp.where(is_a != 0, (slot - (half - 1)) % slots, (half - slot) % slots)


def first_kernel(slots, count_rows, group, plan, scal, keep, *refs):
    half = slots // 2
    blk = refs[0].shape[-1]
    ins, rest = refs[: plan["inputs"]], refs[plan["inputs"] :]
    square, order, fits, dens, pert, sems = rest
    middle, is_a, fit_row, owner = scal[0], scal[1], scal[2], scal[3]

    def first_step(j):
        total = {}
        add_products(slots, total, [("square", dens), ("order", pert)], j + half, dens, j)
        add_products(slots, total, [("order", dens)], j + half, pert, j)
        for s in range(slots):
            kept = keep[j, s] != 0
            square[j, :, cols(s, 1, blk)] = jnp.where(kept, total["square", s], 0.0).astype(jnp.bfloat16)
            order[j, :, cols(s, 1, blk)] = jnp.where(kept, total["order", s], 0.0).astype(jnp.bfloat16)

    def write(s, value):
        value = jnp.where(owner != 0, value, jnp.zeros_like(value))
        fits[place_of(slots, is_a, s)] = value

    @pl.when(middle != 0)
    def _():
        copies = []
        for kind, field, distance, source, start, size, row in plan["moves"]:
            low, high = half - 1 - distance, half + distance
            slot = jnp.where((is_a != 0) == (kind == "near"), low, high)
            target = pert if field else dens
            copies.append(
                pltpu.make_async_copy(
                    ins[source].at[pl.ds(start, size)],
                    target.at[pl.ds(row, size), :, pl.ds(pl.multiple_of(slot * blk, blk), blk)],
                    sems.at[len(copies)],
                )
            )
        for copy in copies:
            copy.start()
        for copy in copies:
            copy.wait()
        in_groups(count_rows + 2 * half - 1, group, first_step)
        response_row(slots, keep, square, order, fit_row, write)


def second_kernel(slots, group, scal, keep, square, order, outs):
    def step(i):
        def write(s, value):
            outs[place_of(slots, scal[1], s), i] = value

        response_row(slots, keep, square, order, i, write)

    @pl.when(scal[0] != 0)
    def _():
        in_groups(outs.shape[1], group, step)


def pack_kernel(pattern, density_in, field_terms, near, far, flags, sems):
    slots, rows = pattern.shape
    half = slots // 2
    my_slot = lax.axis_index("orb")
    first_row = lax.axis_index("aux") * rows
    near_field = jnp.where(my_slot < half, 0, 1)
    copies = [
        pltpu.make_async_copy(pattern, flags, sems.at[0]),
        pltpu.make_async_copy(density_in.at[:, 0], near.at[pl.ds(0, rows)], sems.at[1]),
        pltpu.make_async_copy(density_in.at[:, 0], far.at[pl.ds(0, rows)], sems.at[2]),
        pltpu.make_async_copy(field_terms.at[near_field, :, 0], near.at[pl.ds(rows, rows)], sems.at[3]),
        pltpu.make_async_copy(field_terms.at[1 - near_field, :, 0], far.at[pl.ds(rows, rows)], sems.at[4]),
    ]
    for copy in copies:
        copy.start()
    for copy in copies:
        copy.wait()
    total_rows = lax.axis_size("aux") * rows
    for row in range(rows):
        column = first_row + row + my_slot - half
        kept = (flags[my_slot, row] == 1) & (column >= 0) & (column < total_rows)

        @pl.when(jnp.logical_not(kept))
        def _(row=row):
            for piece in (near, far):
                for place in (row, rows + row):
                    piece[place] = jnp.zeros_like(piece[place])


def preload_kernel(parts, *refs):
    refs, sems = refs[:-1], refs[-1]
    copies = []
    for source, row, rows, column, columns, target, target_row in parts:
        copies.append(
            pltpu.make_async_copy(
                refs[source].at[pl.ds(row, rows), pl.ds(column, columns)],
                refs[target].at[pl.ds(target_row, rows)],
                sems.at[len(copies)],
            )
        )
    for copy in copies:
        copy.start()
    for copy in copies:
        copy.wait()


def sums_kernel(pieces, place, *refs):
    pieces, integrals, out = refs[:pieces], refs[pieces:-1], refs[-1]
    pairs = pieces[0][...]
    for piece in pieces[1:]:
        pairs = pairs + piece[...]
    out[...] = jnp.zeros_like(out)
    fields = pairs.shape[0]
    flat = pairs.reshape(fields, -1)
    start = 0
    for part in integrals:
        width = part.shape[1]
        folds = flat.shape[1] // width
        rows = part.shape[0] // folds
        lhs = [flat[:, fold * width : (fold + 1) * width] for fold in range(folds)]
        lhs = lhs[0] if folds == 1 else jnp.concatenate(lhs, 0)
        value = lax.dot_general(
            lhs, part[...], (((1,), (1,)), ((), ())), preferred_element_type=jnp.float32
        )
        total = value[:fields, :rows]
        for fold in range(1, folds):
            total = total + value[fold * fields : (fold + 1) * fields, fold * rows : (fold + 1) * rows]
        out[place[0], :, start : start + rows] = total
        start += rows


def metric_kernel(*refs):
    pieces, (metric, out) = refs[:-2], refs[-2:]
    sums = pieces[0][...]
    for piece in pieces[1:]:
        sums = sums + piece[...]
    groups, fields, width = sums.shape
    lanes = 128
    totals = [jnp.zeros((out.shape[1], lanes), jnp.float32) for _ in range(fields)]
    full = [
        jnp.concatenate([sums[group, field : field + 1, :] for group in range(groups)], 1)
        for field in range(fields)
    ]
    for start in range(0, groups * width, lanes):
        tile = metric[:, start : start + lanes]
        for field in range(fields):
            totals[field] = totals[field] + tile * full[field][:, start : start + lanes]
    for field in range(fields):
        out[field, :] = jnp.sum(totals[field].T, axis=0)


def on_device(band_pattern, density_in, field_terms, fit_blocks, tensor, metric_inv):
    count_rows = density_in.shape[0]
    blk = density_in.shape[-1]
    fields = field_terms.shape[0]
    slots = lax.axis_size("orb")
    half = slots // 2
    aux_count = lax.axis_size("aux")
    total_rows = count_rows * aux_count
    my_aux = lax.axis_index("aux")
    my_slot = lax.axis_index("orb")
    first_row = my_aux * count_rows
    side_a, side_b = half - 1, half
    is_a = my_slot < half
    middle = (my_slot == side_a) | (my_slot == side_b)
    zero_half = jnp.zeros((), jnp.bfloat16)
    up_rows, down_rows = 2 * half, 2 * half - 2
    forward = [(i, i + 1) for i in range(aux_count - 1)]
    backward = [(i + 1, i) for i in range(aux_count - 1)]

    near, far = pl.pallas_call(
        pack_kernel,
        out_shape=[jax.ShapeDtypeStruct((2 * count_rows, blk, blk), jnp.bfloat16)] * 2,
        in_specs=[pl.BlockSpec(memory_space=pltpu.HBM)] * 3,
        out_specs=[VMEM] * 2,
        scratch_shapes=[pltpu.SMEM((slots, count_rows), jnp.int32), pltpu.SemaphoreType.DMA((5,))],
        compiler_params=pltpu.CompilerParams(vmem_limit_bytes=4 << 20),
        name="pack",
    )(
        *(
            pltpu.with_memory_space_constraint(value, pltpu.HBM)
            for value in (band_pattern.T, density_in, field_terms)
        ),
    )

    inputs, moves = [], []

    def stage_rims(pieces, extra=None):
        split = lambda rows: (rows[:count_rows], rows[count_rows:])
        low = [part[count_rows - up_rows :] for _, _, rows in pieces for part in split(rows)]
        high = [part[:down_rows] for _, _, rows in pieces for part in split(rows)]
        if extra is not None:
            low, high = low + [extra], high + [extra]
        low = lax.ppermute(jnp.concatenate(low, 0), "aux", forward)
        high = lax.ppermute(jnp.concatenate(high, 0), "aux", backward)
        for source, size, row in ((low, up_rows, 0), (high, down_rows, up_rows + count_rows)):
            for index, (kind, distance, _) in enumerate(pieces):
                for field in range(2):
                    start = (2 * index + field) * size
                    moves.append((kind, field, distance, len(inputs), start, size, row))
            inputs.append(source)
        for kind, distance, rows in pieces:
            for field in range(2):
                moves.append((kind, field, distance, len(inputs), field * count_rows, count_rows, up_rows))
            inputs.append(rows)
        return low, high

    wanted = [(my_slot - side_a) % slots, (side_b - my_slot) % slots]
    wanted += [(my_slot - plane) % slots for plane in range(slots)]
    wanted = [[index == step for step in range(slots)] for index in wanted]

    near_got, far_got = {0: near}, {}
    for distance in range(half):
        if distance:
            near_got[distance] = lax.ppermute(near, "orb", [(side_a - distance, side_a), (side_b + distance, side_b)])
        far_got[distance] = lax.ppermute(
            far, "orb", [(side_a - distance, side_b), (side_b + distance, side_a)]
        )
    pattern = jnp.pad(
        band_pattern.astype(jnp.bfloat16), ((0, blk - count_rows), (0, blk - slots))
    )[None]
    low, high = stage_rims([("near", 0, near)], pattern)
    source, metric_source, *flags = lax.optimization_barrier(
        [tensor, metric_inv] + [flag for group in wanted for flag in group]
    )
    wanted = [flags[index : index + slots] for index in range(0, len(flags), slots)]
    source, metric_source = (
        pltpu.with_memory_space_constraint(value, pltpu.HBM)
        for value in (source.reshape(tensor.shape[1], -1), metric_source[0])
    )
    aux_rows, length = source.shape
    whole_rows = aux_rows // 256 * 256
    rest_rows = aux_rows - whole_rows
    folds = 2 if rest_rows <= 128 else 1

    def preload(sources, shapes, parts):
        held = pl.pallas_call(
            functools.partial(preload_kernel, parts),
            out_shape=shapes,
            in_specs=[pl.BlockSpec(memory_space=pltpu.HBM)] * len(sources),
            out_specs=[VMEM] * len(shapes),
            scratch_shapes=[pltpu.SemaphoreType.DMA((len(parts),))],
            compiler_params=pltpu.CompilerParams(vmem_limit_bytes=4 << 20),
        )(*sources)
        return [pltpu.with_memory_space_constraint(value, pltpu.VMEM) for value in held]

    def strips(index, start, rows, column, columns, target, target_row):
        count = max(count for count in (1, 2, 4, 8) if rows % (16 * count) == 0)
        height = rows // count
        return [
            (index, start + strip * height, height, column, columns, target, target_row + strip * height)
            for strip in range(count)
        ]

    integrals = []
    if whole_rows:
        integrals += preload(
            [source],
            [jax.ShapeDtypeStruct((whole_rows, length), source.dtype)],
            strips(0, 0, whole_rows, 0, length, 1, 0),
        )
    (metric,) = preload(
        [metric_source],
        [jax.ShapeDtypeStruct(metric_source.shape, metric_source.dtype)],
        strips(0, 0, metric_source.shape[0], 0, metric_source.shape[1], 1, 0),
    )
    if rest_rows:
        width = length // folds
        parts = []
        for fold in range(folds):
            parts += strips(0, whole_rows, rest_rows, fold * width, width, 1, fold * rest_rows)
        integrals += preload([source], [jax.ShapeDtypeStruct((folds * rest_rows, width), source.dtype)], parts)
    pattern_low = low[-1, count_rows - half : count_rows, :slots].astype(jnp.int32)
    pattern_high = high[-1, : half - 1, :slots].astype(jnp.int32)
    for distance in range(1, half):
        stage_rims(
            [("near", distance, near_got[distance]), ("far", distance - 1, far_got[distance - 1])]
        )
    stage_rims([("far", half - 1, far_got[half - 1])])

    pattern_wide = jnp.concatenate([pattern_low, band_pattern, pattern_high], 0)
    keep_wide = band_keep(pattern_wide, first_row - half, total_rows).astype(jnp.int32)
    owner = fit_blocks[0] // count_rows == my_aux
    scal = jnp.stack(
        [middle.astype(jnp.int32), is_a.astype(jnp.int32), fit_blocks[0] % count_rows, owner.astype(jnp.int32)]
    )
    wide_rows = count_rows + up_rows + down_rows
    mid_rows = count_rows + 2 * half - 1
    plan = {"inputs": len(inputs), "moves": tuple(moves)}
    group = 4 if slots <= 4 else 1
    bands = jax.ShapeDtypeStruct((mid_rows, blk, slots * blk), jnp.bfloat16)
    wide_band = pltpu.VMEM((wide_rows, blk, slots * blk), jnp.bfloat16)
    blocks = 2 * wide_rows * slots
    square, order, fit_parts = pl.pallas_call(
        functools.partial(first_kernel, slots, count_rows, group, plan),
        out_shape=[bands, bands, jax.ShapeDtypeStruct((slots, blk, blk), jnp.bfloat16)],
        in_specs=[SMEM, SMEM] + [ANY] * len(inputs),
        out_specs=[VMEM] * 3,
        scratch_shapes=[wide_band, wide_band, pltpu.SemaphoreType.DMA((len(moves),))],
        compiler_params=pltpu.CompilerParams(vmem_limit_bytes=blocks * blk * blk * 2 + (4 << 20)),
        name="mid_products",
    )(scal, keep_wide, *inputs)
    square, order = (pltpu.with_memory_space_constraint(value, pltpu.VMEM) for value in (square, order))
    parts = pl.pallas_call(
        functools.partial(second_kernel, slots, group),
        out_shape=jax.ShapeDtypeStruct((slots, count_rows, blk, blk), jnp.bfloat16),
        in_specs=[SMEM, SMEM, VMEM, VMEM],
        out_specs=VMEM,
        compiler_params=pltpu.CompilerParams(vmem_limit_bytes=4 << 20),
        name="mid_second",
    )(scal, keep_wide, square, order)

    def scatter(blocks):
        got = [blocks[0]]
        for step in range(1, slots):
            pairs = [(side_a, (side_a + step) % slots), (side_b, (side_b - step) % slots)]
            got.append(lax.ppermute(blocks[step], "orb", pairs))
        return got

    def assemble(got):
        picked = []
        for flags in wanted[:fields]:
            value = got[0]
            for step in range(1, slots):
                value = jnp.where(flags[step], got[step], value)
            picked.append(value)
        return jnp.stack(picked, 0)

    fit_own = assemble(scatter(fit_parts))
    got = scatter(parts)
    response = assemble(got)[:, :, None]
    fit_own = fit_own + lax.ppermute(fit_own, "aux", swap_pairs(aux_count, 1))
    fit_pieces = [fit_own] + [
        lax.ppermute(fit_own, "aux", swap_pairs(aux_count, distance)) for distance in range(2, aux_count, 2)
    ]

    sums = pl.pallas_call(
        functools.partial(sums_kernel, len(fit_pieces)),
        out_shape=jax.ShapeDtypeStruct((aux_count, fields, aux_rows), jnp.float32),
        in_specs=[SMEM] + [VMEM] * (len(fit_pieces) + len(integrals)),
        out_specs=VMEM,
        compiler_params=pltpu.CompilerParams(vmem_limit_bytes=8 << 20),
        name="fit_sums",
    )(my_aux.astype(jnp.int32)[None], *fit_pieces, *integrals)
    sums = sums + lax.ppermute(sums, "aux", swap_pairs(aux_count, 1))
    pieces = [sums] + [
        lax.ppermute(sums, "aux", swap_pairs(aux_count, distance)) for distance in range(2, aux_count, 2)
    ]
    part = pl.pallas_call(
        metric_kernel,
        out_shape=jax.ShapeDtypeStruct((fields, metric.shape[0]), jnp.float32),
        in_specs=[VMEM] * (len(pieces) + 1),
        out_specs=VMEM,
        compiler_params=pltpu.CompilerParams(vmem_limit_bytes=8 << 20),
        name="metric",
    )(*pieces, metric)
    got = [part] + [
        lax.ppermute(part, "orb", [(i, (i + step) % slots) for i in range(slots)]) for step in range(1, slots)
    ]
    coefficients = None
    for plane in range(slots):
        value = got[0]
        for step in range(1, slots):
            value = jnp.where(wanted[fields + plane][step], got[step], value)
        coefficients = value if coefficients is None else coefficients + value
    return (response, coefficients[None])


def solution(mesh):
    in_specs = (
        P("aux", None),
        P("aux", "orb", None, None),
        P(None, "aux", "orb", None, None),
        P(),
        P(None, "aux", "orb", None),
        P(None, "aux", None),
    )
    out_specs = (P(None, "aux", "orb", None, None), P(None, None, "aux"))

    return jax.shard_map(on_device, mesh=mesh, in_specs=in_specs, out_specs=out_specs, check_vma=False)
```

```python
import functools

import jax
import jax.numpy as jnp
from jax import lax
from jax.experimental import pallas as pl
from jax.experimental.pallas import tpu as pltpu
from jax.sharding import PartitionSpec as P


ANY = pl.BlockSpec(memory_space=pl.ANY)
SMEM = pl.BlockSpec(memory_space=pltpu.SMEM)
VMEM = pl.BlockSpec(memory_space=pltpu.VMEM)


def band_keep(band_pattern, first_row, total_rows):
    slot_count = band_pattern.shape[1]
    half_band = slot_count // 2
    row_ids = first_row + jnp.arange(band_pattern.shape[0], dtype=jnp.int32)[:, None]
    columns = row_ids + jnp.arange(slot_count, dtype=jnp.int32)[None, :] - half_band
    return (band_pattern == 1) & (columns >= 0) & (columns < total_rows)


def swap_pairs(count, distance):
    return [(i, i ^ distance) for i in range(count)]


def in_groups(count, group, step):
    group = min(group, count)
    trips = -(-count // group)
    if trips == 1:
        for place in range(count):
            step(place)
        return

    def body(trip, carry):
        start = jnp.minimum(trip * group, count - group)
        for place in range(group):
            step(start + place)
        return carry

    lax.fori_loop(0, trips, body, 0)


def cols(slot, width, blk):
    return pl.ds(slot * blk, width * blk)


def wide(ref, row, low, high, head, tail):
    blk = ref.shape[1]
    parts = [ref[row, :, cols(low, high - low, blk)]]
    if head:
        parts.insert(0, jnp.zeros((blk, head * blk), jnp.bfloat16))
    if tail:
        parts.append(jnp.zeros((blk, tail * blk), jnp.bfloat16))
    return parts[0] if len(parts) == 1 else jnp.concatenate(parts, 1)


def add_products(slots, total, lefts, left_row, right, right_row):
    half, blk = slots // 2, right.shape[1]
    for first in range(0, slots, 2):
        rows, spans = [], []
        for t in (first, first + 1):
            low, high = max(0, t - half), min(slots - 1, slots - 1 + t - half)
            spans.append((t, low, high))
        start, stop = min(v[1] for v in spans), max(v[2] for v in spans)
        for t, low, high in spans:
            u = low - t + half
            rows.append(
                wide(right, right_row + t, u, u + high - low + 1, low - start, stop - high)
            )
        lhs = [left[left_row, :, cols(first, 2, blk)] for _, left in lefts]
        lhs = lhs[0] if len(lhs) == 1 else jnp.concatenate(lhs, 0)
        value = jnp.dot(lhs, jnp.concatenate(rows, 0), preferred_element_type=jnp.float32)
        for index, (key, _) in enumerate(lefts):
            for s in range(start, stop + 1):
                part = value[index * blk : (index + 1) * blk, (s - start) * blk : (s - start + 1) * blk]
                total[key, s] = total[key, s] + part if (key, s) in total else part


def response_row(slots, keep, square, order, i, write):
    half, blk = slots // 2, square.shape[1]
    j = i + half
    total = {}
    add_products(slots, total, [("second", square)], j, order, i)
    add_products(slots, total, [("second", order)], j, square, i)
    for s in range(slots):
        twice = 2.0 * order[j, :, cols(s, 1, blk)].astype(jnp.float32)
        write(s, jnp.where(keep[j, s] != 0, twice - total["second", s], 0.0).astype(jnp.bfloat16))


def place_of(slots, is_a, slot):
    half = slots // 2
    return jnp.where(is_a != 0, (slot - (half - 1)) % slots, (half - slot) % slots)


def first_kernel(slots, count_rows, group, plan, scal, keep, *refs):
    half = slots // 2
    blk = refs[0].shape[-1]
    ins, rest = refs[: plan["inputs"]], refs[plan["inputs"] :]
    square, order, fits, dens, pert, sems = rest
    middle, is_a, fit_row, owner = scal[0], scal[1], scal[2], scal[3]

    def first_step(j):
        total = {}
        add_products(slots, total, [("square", dens), ("order", pert)], j + half, dens, j)
        add_products(slots, total, [("order", dens)], j + half, pert, j)
        for s in range(slots):
            kept = keep[j, s] != 0
            square[j, :, cols(s, 1, blk)] = jnp.where(kept, total["square", s], 0.0).astype(jnp.bfloat16)
            order[j, :, cols(s, 1, blk)] = jnp.where(kept, total["order", s], 0.0).astype(jnp.bfloat16)

    def write(s, value):
        value = jnp.where(owner != 0, value, jnp.zeros_like(value))
        fits[place_of(slots, is_a, s)] = value

    @pl.when(middle != 0)
    def _():
        copies = []
        for kind, field, distance, source, start, size, row in plan["moves"]:
            low, high = half - 1 - distance, half + distance
            slot = jnp.where((is_a != 0) == (kind == "near"), low, high)
            target = pert if field else dens
            copies.append(
                pltpu.make_async_copy(
                    ins[source].at[pl.ds(start, size)],
                    target.at[pl.ds(row, size), :, pl.ds(pl.multiple_of(slot * blk, blk), blk)],
                    sems.at[len(copies)],
                )
            )
        for copy in copies:
            copy.start()
        for copy in copies:
            copy.wait()
        in_groups(count_rows + 2 * half - 1, group, first_step)
        response_row(slots, keep, square, order, fit_row, write)


def second_kernel(slots, group, scal, keep, square, order, outs):
    def step(i):
        def write(s, value):
            outs[place_of(slots, scal[1], s), i] = value

        response_row(slots, keep, square, order, i, write)

    @pl.when(scal[0] != 0)
    def _():
        in_groups(outs.shape[1], group, step)


def pack_kernel(pattern, density_in, field_terms, near, far, flags, sems):
    slots, rows = pattern.shape
    half = slots // 2
    my_slot = lax.axis_index("orb")
    first_row = lax.axis_index("aux") * rows
    near_field = jnp.where(my_slot < half, 0, 1)
    copies = [
        pltpu.make_async_copy(pattern, flags, sems.at[0]),
        pltpu.make_async_copy(density_in.at[:, 0], near.at[pl.ds(0, rows)], sems.at[1]),
        pltpu.make_async_copy(density_in.at[:, 0], far.at[pl.ds(0, rows)], sems.at[2]),
        pltpu.make_async_copy(field_terms.at[near_field, :, 0], near.at[pl.ds(rows, rows)], sems.at[3]),
        pltpu.make_async_copy(field_terms.at[1 - near_field, :, 0], far.at[pl.ds(rows, rows)], sems.at[4]),
    ]
    for copy in copies:
        copy.start()
    for copy in copies:
        copy.wait()
    total_rows = lax.axis_size("aux") * rows
    for row in range(rows):
        column = first_row + row + my_slot - half
        kept = (flags[my_slot, row] == 1) & (column >= 0) & (column < total_rows)

        @pl.when(jnp.logical_not(kept))
        def _(row=row):
            for piece in (near, far):
                for place in (row, rows + row):
                    piece[place] = jnp.zeros_like(piece[place])


def preload_kernel(parts, *refs):
    refs, sems = refs[:-1], refs[-1]
    copies = []
    for source, row, rows, column, columns, target, target_row in parts:
        copies.append(
            pltpu.make_async_copy(
                refs[source].at[pl.ds(row, rows), pl.ds(column, columns)],
                refs[target].at[pl.ds(target_row, rows)],
                sems.at[len(copies)],
            )
        )
    for copy in copies:
        copy.start()
    for copy in copies:
        copy.wait()


def sums_kernel(pieces, place, *refs):
    pieces, integrals, out = refs[:pieces], refs[pieces:-1], refs[-1]
    pairs = pieces[0][...]
    for piece in pieces[1:]:
        pairs = pairs + piece[...]
    out[...] = jnp.zeros_like(out)
    fields = pairs.shape[0]
    flat = pairs.reshape(fields, -1)
    start = 0
    for part in integrals:
        width = part.shape[1]
        folds = flat.shape[1] // width
        rows = part.shape[0] // folds
        lhs = [flat[:, fold * width : (fold + 1) * width] for fold in range(folds)]
        lhs = lhs[0] if folds == 1 else jnp.concatenate(lhs, 0)
        value = lax.dot_general(
            lhs, part[...], (((1,), (1,)), ((), ())), preferred_element_type=jnp.float32
        )
        total = value[:fields, :rows]
        for fold in range(1, folds):
            total = total + value[fold * fields : (fold + 1) * fields, fold * rows : (fold + 1) * rows]
        out[place[0], :, start : start + rows] = total
        start += rows


def metric_kernel(*refs):
    pieces, (metric, out) = refs[:-2], refs[-2:]
    sums = pieces[0][...]
    for piece in pieces[1:]:
        sums = sums + piece[...]
    groups, fields, width = sums.shape
    lanes = 128
    totals = [jnp.zeros((out.shape[1], lanes), jnp.float32) for _ in range(fields)]
    full = [
        jnp.concatenate([sums[group, field : field + 1, :] for group in range(groups)], 1)
        for field in range(fields)
    ]
    for start in range(0, groups * width, lanes):
        tile = metric[:, start : start + lanes]
        for field in range(fields):
            totals[field] = totals[field] + tile * full[field][:, start : start + lanes]
    for field in range(fields):
        out[field, :] = jnp.sum(totals[field].T, axis=0)


def on_device(band_pattern, density_in, field_terms, fit_blocks, tensor, metric_inv):
    count_rows = density_in.shape[0]
    blk = density_in.shape[-1]
    fields = field_terms.shape[0]
    slots = lax.axis_size("orb")
    half = slots // 2
    aux_count = lax.axis_size("aux")
    total_rows = count_rows * aux_count
    my_aux = lax.axis_index("aux")
    my_slot = lax.axis_index("orb")
    first_row = my_aux * count_rows
    side_a, side_b = half - 1, half
    is_a = my_slot < half
    middle = (my_slot == side_a) | (my_slot == side_b)
    zero_half = jnp.zeros((), jnp.bfloat16)
    up_rows, down_rows = 2 * half, 2 * half - 2
    forward = [(i, i + 1) for i in range(aux_count - 1)]
    backward = [(i + 1, i) for i in range(aux_count - 1)]

    near, far = pl.pallas_call(
        pack_kernel,
        out_shape=[jax.ShapeDtypeStruct((2 * count_rows, blk, blk), jnp.bfloat16)] * 2,
        in_specs=[pl.BlockSpec(memory_space=pltpu.HBM)] * 3,
        out_specs=[VMEM] * 2,
        scratch_shapes=[pltpu.SMEM((slots, count_rows), jnp.int32), pltpu.SemaphoreType.DMA((5,))],
        compiler_params=pltpu.CompilerParams(vmem_limit_bytes=4 << 20),
        name="pack",
    )(
        *(
            pltpu.with_memory_space_constraint(value, pltpu.HBM)
            for value in (band_pattern.T, density_in, field_terms)
        ),
    )

    inputs, moves = [], []

    def stage_rims(pieces, extra=None):
        split = lambda rows: (rows[:count_rows], rows[count_rows:])
        low = [part[count_rows - up_rows :] for _, _, rows in pieces for part in split(rows)]
        high = [part[:down_rows] for _, _, rows in pieces for part in split(rows)]
        if extra is not None:
            low, high = low + [extra], high + [extra]
        low = lax.ppermute(jnp.concatenate(low, 0), "aux", forward)
        high = lax.ppermute(jnp.concatenate(high, 0), "aux", backward)
        for source, size, row in ((low, up_rows, 0), (high, down_rows, up_rows + count_rows)):
            for index, (kind, distance, _) in enumerate(pieces):
                for field in range(2):
                    start = (2 * index + field) * size
                    moves.append((kind, field, distance, len(inputs), start, size, row))
            inputs.append(source)
        for kind, distance, rows in pieces:
            for field in range(2):
                moves.append((kind, field, distance, len(inputs), field * count_rows, count_rows, up_rows))
            inputs.append(rows)
        return low, high

    wanted = [(my_slot - side_a) % slots, (side_b - my_slot) % slots]
    wanted += [my_slot ^ plane for plane in range(slots)]
    wanted = [[index == step for step in range(slots)] for index in wanted]

    near_got, far_got = {0: near}, {}
    for distance in range(half):
        if distance:
            near_got[distance] = lax.ppermute(near, "orb", [(side_a - distance, side_a), (side_b + distance, side_b)])
        far_got[distance] = lax.ppermute(
            far, "orb", [(side_a - distance, side_b), (side_b + distance, side_a)]
        )
    pattern = jnp.pad(
        band_pattern.astype(jnp.bfloat16), ((0, blk - count_rows), (0, blk - slots))
    )[None]
    low, high = stage_rims([("near", 0, near)], pattern)
    source, metric_source, *flags = lax.optimization_barrier(
        [tensor, metric_inv] + [flag for group in wanted for flag in group]
    )
    wanted = [flags[index : index + slots] for index in range(0, len(flags), slots)]
    source, metric_source = (
        pltpu.with_memory_space_constraint(value, pltpu.HBM)
        for value in (source.reshape(tensor.shape[1], -1), metric_source[0])
    )
    aux_rows, length = source.shape
    whole_rows = aux_rows // 256 * 256
    rest_rows = aux_rows - whole_rows
    folds = 2 if rest_rows <= 128 else 1

    def preload(sources, shapes, parts):
        held = pl.pallas_call(
            functools.partial(preload_kernel, parts),
            out_shape=shapes,
            in_specs=[pl.BlockSpec(memory_space=pltpu.HBM)] * len(sources),
            out_specs=[VMEM] * len(shapes),
            scratch_shapes=[pltpu.SemaphoreType.DMA((len(parts),))],
            compiler_params=pltpu.CompilerParams(vmem_limit_bytes=4 << 20),
        )(*sources)
        return [pltpu.with_memory_space_constraint(value, pltpu.VMEM) for value in held]

    def strips(index, start, rows, column, columns, target, target_row):
        count = max(count for count in (1, 2, 4, 8) if rows % (16 * count) == 0)
        height = rows // count
        return [
            (index, start + strip * height, height, column, columns, target, target_row + strip * height)
            for strip in range(count)
        ]

    integrals = []
    if whole_rows:
        integrals += preload(
            [source],
            [jax.ShapeDtypeStruct((whole_rows, length), source.dtype)],
            strips(0, 0, whole_rows, 0, length, 1, 0),
        )
    (metric,) = preload(
        [metric_source],
        [jax.ShapeDtypeStruct(metric_source.shape, metric_source.dtype)],
        strips(0, 0, metric_source.shape[0], 0, metric_source.shape[1], 1, 0),
    )
    if rest_rows:
        width = length // folds
        parts = []
        for fold in range(folds):
            parts += strips(0, whole_rows, rest_rows, fold * width, width, 1, fold * rest_rows)
        integrals += preload([source], [jax.ShapeDtypeStruct((folds * rest_rows, width), source.dtype)], parts)
    pattern_low = low[-1, count_rows - half : count_rows, :slots].astype(jnp.int32)
    pattern_high = high[-1, : half - 1, :slots].astype(jnp.int32)
    for distance in range(1, half):
        stage_rims(
            [("near", distance, near_got[distance]), ("far", distance - 1, far_got[distance - 1])]
        )
    stage_rims([("far", half - 1, far_got[half - 1])])

    pattern_wide = jnp.concatenate([pattern_low, band_pattern, pattern_high], 0)
    keep_wide = band_keep(pattern_wide, first_row - half, total_rows).astype(jnp.int32)
    owner = fit_blocks[0] // count_rows == my_aux
    scal = jnp.stack(
        [middle.astype(jnp.int32), is_a.astype(jnp.int32), fit_blocks[0] % count_rows, owner.astype(jnp.int32)]
    )
    wide_rows = count_rows + up_rows + down_rows
    mid_rows = count_rows + 2 * half - 1
    plan = {"inputs": len(inputs), "moves": tuple(moves)}
    group = mid_rows if slots <= 4 else 1
    bands = jax.ShapeDtypeStruct((mid_rows, blk, slots * blk), jnp.bfloat16)
    wide_band = pltpu.VMEM((wide_rows, blk, slots * blk), jnp.bfloat16)
    blocks = 2 * wide_rows * slots
    square, order, fit_parts = pl.pallas_call(
        functools.partial(first_kernel, slots, count_rows, group, plan),
        out_shape=[bands, bands, jax.ShapeDtypeStruct((slots, blk, blk), jnp.bfloat16)],
        in_specs=[SMEM, SMEM] + [ANY] * len(inputs),
        out_specs=[VMEM] * 3,
        scratch_shapes=[wide_band, wide_band, pltpu.SemaphoreType.DMA((len(moves),))],
        compiler_params=pltpu.CompilerParams(vmem_limit_bytes=blocks * blk * blk * 2 + (4 << 20)),
        name="mid_products",
    )(scal, keep_wide, *inputs)
    square, order = (pltpu.with_memory_space_constraint(value, pltpu.VMEM) for value in (square, order))
    parts = pl.pallas_call(
        functools.partial(second_kernel, slots, group),
        out_shape=jax.ShapeDtypeStruct((slots, count_rows, blk, blk), jnp.bfloat16),
        in_specs=[SMEM, SMEM, VMEM, VMEM],
        out_specs=VMEM,
        compiler_params=pltpu.CompilerParams(vmem_limit_bytes=4 << 20),
        name="mid_second",
    )(scal, keep_wide, square, order)

    def scatter(blocks):
        got = [blocks[0]]
        for step in range(1, slots):
            pairs = [(side_a, (side_a + step) % slots), (side_b, (side_b - step) % slots)]
            got.append(lax.ppermute(blocks[step], "orb", pairs))
        return got

    def assemble(got):
        picked = []
        for flags in wanted[:fields]:
            value = got[0]
            for step in range(1, slots):
                value = jnp.where(flags[step], got[step], value)
            picked.append(value)
        return jnp.stack(picked, 0)

    fit_own = assemble(scatter(fit_parts))
    got = scatter(parts)
    response = assemble(got)[:, :, None]
    fit_own = fit_own + lax.ppermute(fit_own, "aux", swap_pairs(aux_count, 1))
    fit_pieces = [fit_own] + [
        lax.ppermute(fit_own, "aux", swap_pairs(aux_count, distance)) for distance in range(2, aux_count, 2)
    ]

    sums = pl.pallas_call(
        functools.partial(sums_kernel, len(fit_pieces)),
        out_shape=jax.ShapeDtypeStruct((aux_count, fields, aux_rows), jnp.float32),
        in_specs=[SMEM] + [VMEM] * (len(fit_pieces) + len(integrals)),
        out_specs=VMEM,
        compiler_params=pltpu.CompilerParams(vmem_limit_bytes=8 << 20),
        name="fit_sums",
    )(my_aux.astype(jnp.int32)[None], *fit_pieces, *integrals)
    sums = sums + lax.ppermute(sums, "aux", swap_pairs(aux_count, 1))
    pieces = [sums] + [
        lax.ppermute(sums, "aux", swap_pairs(aux_count, distance)) for distance in range(2, aux_count, 2)
    ]
    part = pl.pallas_call(
        metric_kernel,
        out_shape=jax.ShapeDtypeStruct((fields, metric.shape[0]), jnp.float32),
        in_specs=[VMEM] * (len(pieces) + 1),
        out_specs=VMEM,
        compiler_params=pltpu.CompilerParams(vmem_limit_bytes=8 << 20),
        name="metric",
    )(*pieces, metric)
    got = [part] * slots
    for distance in range(slots - 1, 0, -1):
        got[distance] = lax.ppermute(part, "orb", swap_pairs(slots, distance))
    coefficients = None
    for plane in range(slots):
        value = got[0]
        for distance in range(1, slots):
            value = jnp.where(wanted[fields + plane][distance], got[distance], value)
        coefficients = value if coefficients is None else coefficients + value
    return (response, coefficients[None])


def solution(mesh):
    in_specs = (
        P("aux", None),
        P("aux", "orb", None, None),
        P(None, "aux", "orb", None, None),
        P(),
        P(None, "aux", "orb", None),
        P(None, "aux", None),
    )
    out_specs = (P(None, "aux", "orb", None, None), P(None, None, "aux"))

    return jax.shard_map(on_device, mesh=mesh, in_specs=in_specs, out_specs=out_specs, check_vma=False)
```

```python
import functools

import jax
import jax.numpy as jnp
from jax import lax
from jax.experimental import pallas as pl
from jax.experimental.pallas import tpu as pltpu
from jax.sharding import PartitionSpec as P


ANY = pl.BlockSpec(memory_space=pl.ANY)
SMEM = pl.BlockSpec(memory_space=pltpu.SMEM)
VMEM = pl.BlockSpec(memory_space=pltpu.VMEM)


def band_keep(band_pattern, first_row, total_rows):
    slot_count = band_pattern.shape[1]
    half_band = slot_count // 2
    row_ids = first_row + jnp.arange(band_pattern.shape[0], dtype=jnp.int32)[:, None]
    columns = row_ids + jnp.arange(slot_count, dtype=jnp.int32)[None, :] - half_band
    return (band_pattern == 1) & (columns >= 0) & (columns < total_rows)


def swap_pairs(count, distance):
    return [(i, i ^ distance) for i in range(count)]


def in_groups(count, group, step):
    group = min(group, count)
    trips = -(-count // group)
    if trips == 1:
        for place in range(count):
            step(place)
        return

    def body(trip, carry):
        start = jnp.minimum(trip * group, count - group)
        for place in range(group):
            step(start + place)
        return carry

    lax.fori_loop(0, trips, body, 0)


def cols(slot, width, blk):
    return pl.ds(slot * blk, width * blk)


def wide(ref, row, low, high, head, tail):
    blk = ref.shape[1]
    parts = [ref[row, :, cols(low, high - low, blk)]]
    if head:
        parts.insert(0, jnp.zeros((blk, head * blk), jnp.bfloat16))
    if tail:
        parts.append(jnp.zeros((blk, tail * blk), jnp.bfloat16))
    return parts[0] if len(parts) == 1 else jnp.concatenate(parts, 1)


def add_products(slots, total, lefts, left_row, right, right_row):
    half, blk = slots // 2, right.shape[1]
    for first in range(0, slots, 2):
        rows, spans = [], []
        for t in (first, first + 1):
            low, high = max(0, t - half), min(slots - 1, slots - 1 + t - half)
            spans.append((t, low, high))
        start, stop = min(v[1] for v in spans), max(v[2] for v in spans)
        for t, low, high in spans:
            u = low - t + half
            rows.append(
                wide(right, right_row + t, u, u + high - low + 1, low - start, stop - high)
            )
        lhs = [left[left_row, :, cols(first, 2, blk)] for _, left in lefts]
        lhs = lhs[0] if len(lhs) == 1 else jnp.concatenate(lhs, 0)
        value = jnp.dot(lhs, jnp.concatenate(rows, 0), preferred_element_type=jnp.float32)
        for index, (key, _) in enumerate(lefts):
            for s in range(start, stop + 1):
                part = value[index * blk : (index + 1) * blk, (s - start) * blk : (s - start + 1) * blk]
                total[key, s] = total[key, s] + part if (key, s) in total else part


def response_row(slots, keep, square, order, i, write):
    half, blk = slots // 2, square.shape[1]
    j = i + half
    total = {}
    add_products(slots, total, [("second", square)], j, order, i)
    add_products(slots, total, [("second", order)], j, square, i)
    for s in range(slots):
        twice = 2.0 * order[j, :, cols(s, 1, blk)].astype(jnp.float32)
        write(s, jnp.where(keep[j, s] != 0, twice - total["second", s], 0.0).astype(jnp.bfloat16))


def place_of(slots, is_a, slot):
    half = slots // 2
    return jnp.where(is_a != 0, (slot - (half - 1)) % slots, (half - slot) % slots)


def first_kernel(slots, count_rows, group, plan, scal, keep, *refs):
    half = slots // 2
    blk = refs[0].shape[-1]
    ins, rest = refs[: plan["inputs"]], refs[plan["inputs"] :]
    square, order, fits, dens, pert, sems = rest
    middle, is_a, fit_row, owner = scal[0], scal[1], scal[2], scal[3]

    def first_step(j):
        total = {}
        add_products(slots, total, [("square", dens), ("order", pert)], j + half, dens, j)
        add_products(slots, total, [("order", dens)], j + half, pert, j)
        for s in range(slots):
            kept = keep[j, s] != 0
            square[j, :, cols(s, 1, blk)] = jnp.where(kept, total["square", s], 0.0).astype(jnp.bfloat16)
            order[j, :, cols(s, 1, blk)] = jnp.where(kept, total["order", s], 0.0).astype(jnp.bfloat16)

    def write(s, value):
        value = jnp.where(owner != 0, value, jnp.zeros_like(value))
        fits[place_of(slots, is_a, s)] = value

    @pl.when(middle != 0)
    def _():
        copies = []
        for kind, field, distance, source, start, size, row in plan["moves"]:
            low, high = half - 1 - distance, half + distance
            slot = jnp.where((is_a != 0) == (kind == "near"), low, high)
            target = pert if field else dens
            copies.append(
                pltpu.make_async_copy(
                    ins[source].at[pl.ds(start, size)],
                    target.at[pl.ds(row, size), :, pl.ds(pl.multiple_of(slot * blk, blk), blk)],
                    sems.at[len(copies)],
                )
            )
        for copy in copies:
            copy.start()
        for copy in copies:
            copy.wait()
        in_groups(count_rows + 2 * half - 1, group, first_step)
        response_row(slots, keep, square, order, fit_row, write)


def second_kernel(slots, group, scal, keep, square, order, outs):
    def step(i):
        def write(s, value):
            outs[place_of(slots, scal[1], s), i] = value

        response_row(slots, keep, square, order, i, write)

    @pl.when(scal[0] != 0)
    def _():
        in_groups(outs.shape[1], group, step)


def pack_kernel(pattern, density_in, field_terms, near, far, flags, sems):
    slots, rows = pattern.shape
    half = slots // 2
    my_slot = lax.axis_index("orb")
    first_row = lax.axis_index("aux") * rows
    near_field = jnp.where(my_slot < half, 0, 1)
    copies = [
        pltpu.make_async_copy(pattern, flags, sems.at[0]),
        pltpu.make_async_copy(density_in.at[:, 0], near.at[pl.ds(0, rows)], sems.at[1]),
        pltpu.make_async_copy(density_in.at[:, 0], far.at[pl.ds(0, rows)], sems.at[2]),
        pltpu.make_async_copy(field_terms.at[near_field, :, 0], near.at[pl.ds(rows, rows)], sems.at[3]),
        pltpu.make_async_copy(field_terms.at[1 - near_field, :, 0], far.at[pl.ds(rows, rows)], sems.at[4]),
    ]
    for copy in copies:
        copy.start()
    for copy in copies:
        copy.wait()
    total_rows = lax.axis_size("aux") * rows
    for row in range(rows):
        column = first_row + row + my_slot - half
        kept = (flags[my_slot, row] == 1) & (column >= 0) & (column < total_rows)

        @pl.when(jnp.logical_not(kept))
        def _(row=row):
            for piece in (near, far):
                for place in (row, rows + row):
                    piece[place] = jnp.zeros_like(piece[place])


def preload_kernel(parts, *refs):
    refs, sems = refs[:-1], refs[-1]
    copies = []
    for source, row, rows, column, columns, target, target_row in parts:
        copies.append(
            pltpu.make_async_copy(
                refs[source].at[pl.ds(row, rows), pl.ds(column, columns)],
                refs[target].at[pl.ds(target_row, rows)],
                sems.at[len(copies)],
            )
        )
    for copy in copies:
        copy.start()
    for copy in copies:
        copy.wait()


def sums_kernel(pieces, place, *refs):
    pieces, integrals, out = refs[:pieces], refs[pieces:-1], refs[-1]
    pairs = pieces[0][...]
    for piece in pieces[1:]:
        pairs = pairs + piece[...]
    out[...] = jnp.zeros_like(out)
    fields = pairs.shape[0]
    flat = pairs.reshape(fields, -1)
    start = 0
    for part in integrals:
        width = part.shape[1]
        folds = flat.shape[1] // width
        rows = part.shape[0] // folds
        lhs = [flat[:, fold * width : (fold + 1) * width] for fold in range(folds)]
        lhs = lhs[0] if folds == 1 else jnp.concatenate(lhs, 0)
        value = lax.dot_general(
            lhs, part[...], (((1,), (1,)), ((), ())), preferred_element_type=jnp.float32
        )
        total = value[:fields, :rows]
        for fold in range(1, folds):
            total = total + value[fold * fields : (fold + 1) * fields, fold * rows : (fold + 1) * rows]
        out[place[0], :, start : start + rows] = total
        start += rows


def metric_kernel(*refs):
    pieces, (metric, out) = refs[:-2], refs[-2:]
    sums = pieces[0][...]
    for piece in pieces[1:]:
        sums = sums + piece[...]
    groups, fields, width = sums.shape
    lanes = 128
    totals = [jnp.zeros((out.shape[1], lanes), jnp.float32) for _ in range(fields)]
    full = [
        jnp.concatenate([sums[group, field : field + 1, :] for group in range(groups)], 1)
        for field in range(fields)
    ]
    for start in range(0, groups * width, lanes):
        tile = metric[:, start : start + lanes]
        for field in range(fields):
            totals[field] = totals[field] + tile * full[field][:, start : start + lanes]
    for field in range(fields):
        out[field, :] = jnp.sum(totals[field].T, axis=0)


def on_device(band_pattern, density_in, field_terms, fit_blocks, tensor, metric_inv):
    count_rows = density_in.shape[0]
    blk = density_in.shape[-1]
    fields = field_terms.shape[0]
    slots = lax.axis_size("orb")
    half = slots // 2
    aux_count = lax.axis_size("aux")
    total_rows = count_rows * aux_count
    my_aux = lax.axis_index("aux")
    my_slot = lax.axis_index("orb")
    first_row = my_aux * count_rows
    side_a, side_b = half - 1, half
    is_a = my_slot < half
    middle = (my_slot == side_a) | (my_slot == side_b)
    zero_half = jnp.zeros((), jnp.bfloat16)
    up_rows, down_rows = 2 * half, 2 * half - 2
    forward = [
        (i * slots + side, (i + 1) * slots + side) for i in range(aux_count - 1) for side in (side_a, side_b)
    ]
    backward = [(target, source) for source, target in forward]

    near, far = pl.pallas_call(
        pack_kernel,
        out_shape=[jax.ShapeDtypeStruct((2 * count_rows, blk, blk), jnp.bfloat16)] * 2,
        in_specs=[pl.BlockSpec(memory_space=pltpu.HBM)] * 3,
        out_specs=[VMEM] * 2,
        scratch_shapes=[pltpu.SMEM((slots, count_rows), jnp.int32), pltpu.SemaphoreType.DMA((5,))],
        compiler_params=pltpu.CompilerParams(vmem_limit_bytes=4 << 20),
        name="pack",
    )(
        *(
            pltpu.with_memory_space_constraint(value, pltpu.HBM)
            for value in (band_pattern.T, density_in, field_terms)
        ),
    )

    inputs, moves = [], []

    def stage_rims(pieces, extra=None):
        split = lambda rows: (rows[:count_rows], rows[count_rows:])
        low = [part[count_rows - up_rows :] for _, _, rows in pieces for part in split(rows)]
        high = [part[:down_rows] for _, _, rows in pieces for part in split(rows)]
        if extra is not None:
            low, high = low + [extra], high + [extra]
        low = lax.ppermute(jnp.concatenate(low, 0), ("aux", "orb"), forward)
        high = lax.ppermute(jnp.concatenate(high, 0), ("aux", "orb"), backward)
        for source, size, row in ((low, up_rows, 0), (high, down_rows, up_rows + count_rows)):
            for index, (kind, distance, _) in enumerate(pieces):
                for field in range(2):
                    start = (2 * index + field) * size
                    moves.append((kind, field, distance, len(inputs), start, size, row))
            inputs.append(source)
        for kind, distance, rows in pieces:
            for field in range(2):
                moves.append((kind, field, distance, len(inputs), field * count_rows, count_rows, up_rows))
            inputs.append(rows)
        return low, high

    wanted = [(my_slot - side_a) % slots, (side_b - my_slot) % slots]
    wanted += [my_slot ^ plane for plane in range(slots)]
    wanted = [[index == step for step in range(slots)] for index in wanted]

    near_got, far_got = {0: near}, {}
    for distance in range(half):
        if distance:
            near_got[distance] = lax.ppermute(near, "orb", [(side_a - distance, side_a), (side_b + distance, side_b)])
        far_got[distance] = lax.ppermute(
            far, "orb", [(side_a - distance, side_b), (side_b + distance, side_a)]
        )
    pattern = jnp.pad(
        band_pattern.astype(jnp.bfloat16), ((0, blk - count_rows), (0, blk - slots))
    )[None]
    low, high = stage_rims([("near", 0, near)], pattern)
    source, metric_source, *flags = lax.optimization_barrier(
        [tensor, metric_inv] + [flag for group in wanted for flag in group]
    )
    wanted = [flags[index : index + slots] for index in range(0, len(flags), slots)]
    source, metric_source = (
        pltpu.with_memory_space_constraint(value, pltpu.HBM)
        for value in (source.reshape(tensor.shape[1], -1), metric_source[0])
    )
    aux_rows, length = source.shape
    whole_rows = aux_rows // 256 * 256
    rest_rows = aux_rows - whole_rows
    folds = 2 if rest_rows <= 128 else 1

    def preload(sources, shapes, parts):
        held = pl.pallas_call(
            functools.partial(preload_kernel, parts),
            out_shape=shapes,
            in_specs=[pl.BlockSpec(memory_space=pltpu.HBM)] * len(sources),
            out_specs=[VMEM] * len(shapes),
            scratch_shapes=[pltpu.SemaphoreType.DMA((len(parts),))],
            compiler_params=pltpu.CompilerParams(vmem_limit_bytes=4 << 20),
        )(*sources)
        return [pltpu.with_memory_space_constraint(value, pltpu.VMEM) for value in held]

    def strips(index, start, rows, column, columns, target, target_row):
        count = max(count for count in (1, 2, 4, 8) if rows % (16 * count) == 0)
        height = rows // count
        return [
            (index, start + strip * height, height, column, columns, target, target_row + strip * height)
            for strip in range(count)
        ]

    integrals = []
    if whole_rows:
        integrals += preload(
            [source],
            [jax.ShapeDtypeStruct((whole_rows, length), source.dtype)],
            strips(0, 0, whole_rows, 0, length, 1, 0),
        )
    (metric,) = preload(
        [metric_source],
        [jax.ShapeDtypeStruct(metric_source.shape, metric_source.dtype)],
        strips(0, 0, metric_source.shape[0], 0, metric_source.shape[1], 1, 0),
    )
    if rest_rows:
        width = length // folds
        parts = []
        for fold in range(folds):
            parts += strips(0, whole_rows, rest_rows, fold * width, width, 1, fold * rest_rows)
        integrals += preload([source], [jax.ShapeDtypeStruct((folds * rest_rows, width), source.dtype)], parts)
    pattern_low = low[-1, count_rows - half : count_rows, :slots].astype(jnp.int32)
    pattern_high = high[-1, : half - 1, :slots].astype(jnp.int32)
    for distance in range(1, half):
        stage_rims(
            [("near", distance, near_got[distance]), ("far", distance - 1, far_got[distance - 1])]
        )
    stage_rims([("far", half - 1, far_got[half - 1])])

    pattern_wide = jnp.concatenate([pattern_low, band_pattern, pattern_high], 0)
    keep_wide = band_keep(pattern_wide, first_row - half, total_rows).astype(jnp.int32)
    owner = fit_blocks[0] // count_rows == my_aux
    scal = jnp.stack(
        [middle.astype(jnp.int32), is_a.astype(jnp.int32), fit_blocks[0] % count_rows, owner.astype(jnp.int32)]
    )
    wide_rows = count_rows + up_rows + down_rows
    mid_rows = count_rows + 2 * half - 1
    plan = {"inputs": len(inputs), "moves": tuple(moves)}
    group = mid_rows if slots <= 4 else 1
    bands = jax.ShapeDtypeStruct((mid_rows, blk, slots * blk), jnp.bfloat16)
    wide_band = pltpu.VMEM((wide_rows, blk, slots * blk), jnp.bfloat16)
    blocks = 2 * wide_rows * slots
    square, order, fit_parts = pl.pallas_call(
        functools.partial(first_kernel, slots, count_rows, group, plan),
        out_shape=[bands, bands, jax.ShapeDtypeStruct((slots, blk, blk), jnp.bfloat16)],
        in_specs=[SMEM, SMEM] + [ANY] * len(inputs),
        out_specs=[VMEM] * 3,
        scratch_shapes=[wide_band, wide_band, pltpu.SemaphoreType.DMA((len(moves),))],
        compiler_params=pltpu.CompilerParams(vmem_limit_bytes=blocks * blk * blk * 2 + (4 << 20)),
        name="mid_products",
    )(scal, keep_wide, *inputs)
    square, order = (pltpu.with_memory_space_constraint(value, pltpu.VMEM) for value in (square, order))
    parts = pl.pallas_call(
        functools.partial(second_kernel, slots, group),
        out_shape=jax.ShapeDtypeStruct((slots, count_rows, blk, blk), jnp.bfloat16),
        in_specs=[SMEM, SMEM, VMEM, VMEM],
        out_specs=VMEM,
        compiler_params=pltpu.CompilerParams(vmem_limit_bytes=4 << 20),
        name="mid_second",
    )(scal, keep_wide, square, order)

    def scatter(blocks):
        got = [blocks[0]]
        for step in range(1, slots):
            pairs = [(side_a, (side_a + step) % slots), (side_b, (side_b - step) % slots)]
            got.append(lax.ppermute(blocks[step], "orb", pairs))
        return got

    def assemble(got):
        picked = []
        for flags in wanted[:fields]:
            value = got[0]
            for step in range(1, slots):
                value = jnp.where(flags[step], got[step], value)
            picked.append(value)
        return jnp.stack(picked, 0)

    fit_own = assemble(scatter(fit_parts))
    got = scatter(parts)
    response = assemble(got)[:, :, None]
    fit_own = fit_own + lax.ppermute(fit_own, "aux", swap_pairs(aux_count, 1))
    fit_pieces = [fit_own] + [
        lax.ppermute(fit_own, "aux", swap_pairs(aux_count, distance)) for distance in range(2, aux_count, 2)
    ]

    sums = pl.pallas_call(
        functools.partial(sums_kernel, len(fit_pieces)),
        out_shape=jax.ShapeDtypeStruct((aux_count, fields, aux_rows), jnp.float32),
        in_specs=[SMEM] + [VMEM] * (len(fit_pieces) + len(integrals)),
        out_specs=VMEM,
        compiler_params=pltpu.CompilerParams(vmem_limit_bytes=8 << 20),
        name="fit_sums",
    )(my_aux.astype(jnp.int32)[None], *fit_pieces, *integrals)
    sums = sums + lax.ppermute(sums, "aux", swap_pairs(aux_count, 1))
    pieces = [sums] + [
        lax.ppermute(sums, "aux", swap_pairs(aux_count, distance)) for distance in range(2, aux_count, 2)
    ]
    part = pl.pallas_call(
        metric_kernel,
        out_shape=jax.ShapeDtypeStruct((fields, metric.shape[0]), jnp.float32),
        in_specs=[VMEM] * (len(pieces) + 1),
        out_specs=VMEM,
        compiler_params=pltpu.CompilerParams(vmem_limit_bytes=8 << 20),
        name="metric",
    )(*pieces, metric)
    got = [part] * slots
    for distance in range(slots - 1, 0, -1):
        got[distance] = lax.ppermute(part, "orb", swap_pairs(slots, distance))
    coefficients = None
    for plane in range(slots):
        value = got[0]
        for distance in range(1, slots):
            value = jnp.where(wanted[fields + plane][distance], got[distance], value)
        coefficients = value if coefficients is None else coefficients + value
    return (response, coefficients[None])


def solution(mesh):
    in_specs = (
        P("aux", None),
        P("aux", "orb", None, None),
        P(None, "aux", "orb", None, None),
        P(),
        P(None, "aux", "orb", None),
        P(None, "aux", None),
    )
    out_specs = (P(None, "aux", "orb", None, None), P(None, None, "aux"))

    return jax.shard_map(on_device, mesh=mesh, in_specs=in_specs, out_specs=out_specs, check_vma=False)
```

```python
import functools

import jax
import jax.numpy as jnp
from jax import lax
from jax.experimental import pallas as pl
from jax.experimental.pallas import tpu as pltpu
from jax.sharding import PartitionSpec as P


ANY = pl.BlockSpec(memory_space=pl.ANY)
SMEM = pl.BlockSpec(memory_space=pltpu.SMEM)
VMEM = pl.BlockSpec(memory_space=pltpu.VMEM)


def band_keep(band_pattern, first_row, total_rows):
    slot_count = band_pattern.shape[1]
    half_band = slot_count // 2
    row_ids = first_row + jnp.arange(band_pattern.shape[0], dtype=jnp.int32)[:, None]
    columns = row_ids + jnp.arange(slot_count, dtype=jnp.int32)[None, :] - half_band
    return (band_pattern == 1) & (columns >= 0) & (columns < total_rows)


def swap_pairs(count, distance):
    return [(i, i ^ distance) for i in range(count)]


def in_groups(count, group, step):
    group = min(group, count)
    trips = -(-count // group)
    if trips == 1:
        for place in range(count):
            step(place)
        return

    def body(trip, carry):
        start = jnp.minimum(trip * group, count - group)
        for place in range(group):
            step(start + place)
        return carry

    lax.fori_loop(0, trips, body, 0)


def cols(slot, width, blk):
    return pl.ds(slot * blk, width * blk)


def wide(ref, row, low, high, head, tail):
    blk = ref.shape[1]
    parts = [ref[row, :, cols(low, high - low, blk)]]
    if head:
        parts.insert(0, jnp.zeros((blk, head * blk), jnp.bfloat16))
    if tail:
        parts.append(jnp.zeros((blk, tail * blk), jnp.bfloat16))
    return parts[0] if len(parts) == 1 else jnp.concatenate(parts, 1)


def add_products(slots, total, lefts, left_row, right, right_row):
    half, blk = slots // 2, right.shape[1]
    for first in range(0, slots, 2):
        rows, spans = [], []
        for t in (first, first + 1):
            low, high = max(0, t - half), min(slots - 1, slots - 1 + t - half)
            spans.append((t, low, high))
        start, stop = min(v[1] for v in spans), max(v[2] for v in spans)
        for t, low, high in spans:
            u = low - t + half
            rows.append(
                wide(right, right_row + t, u, u + high - low + 1, low - start, stop - high)
            )
        lhs = [left[left_row, :, cols(first, 2, blk)] for _, left in lefts]
        lhs = lhs[0] if len(lhs) == 1 else jnp.concatenate(lhs, 0)
        value = jnp.dot(lhs, jnp.concatenate(rows, 0), preferred_element_type=jnp.float32)
        for index, (key, _) in enumerate(lefts):
            for s in range(start, stop + 1):
                part = value[index * blk : (index + 1) * blk, (s - start) * blk : (s - start + 1) * blk]
                total[key, s] = total[key, s] + part if (key, s) in total else part


def response_row(slots, keep, square, order, i, write):
    half, blk = slots // 2, square.shape[1]
    j = i + half
    total = {}
    add_products(slots, total, [("second", square)], j, order, i)
    add_products(slots, total, [("second", order)], j, square, i)
    for s in range(slots):
        twice = 2.0 * order[j, :, cols(s, 1, blk)].astype(jnp.float32)
        write(s, jnp.where(keep[j, s] != 0, twice - total["second", s], 0.0).astype(jnp.bfloat16))


def place_of(slots, is_a, slot):
    half = slots // 2
    return jnp.where(is_a != 0, (slot - (half - 1)) % slots, (half - slot) % slots)


def first_kernel(slots, count_rows, group, plan, scal, keep, *refs):
    half = slots // 2
    blk = refs[0].shape[-1]
    ins, rest = refs[: plan["inputs"]], refs[plan["inputs"] :]
    square, order, fits, dens, pert, sems = rest
    middle, is_a, fit_row, owner = scal[0], scal[1], scal[2], scal[3]

    def first_step(j):
        total = {}
        add_products(slots, total, [("square", dens), ("order", pert)], j + half, dens, j)
        add_products(slots, total, [("order", dens)], j + half, pert, j)
        for s in range(slots):
            kept = keep[j, s] != 0
            square[j, :, cols(s, 1, blk)] = jnp.where(kept, total["square", s], 0.0).astype(jnp.bfloat16)
            order[j, :, cols(s, 1, blk)] = jnp.where(kept, total["order", s], 0.0).astype(jnp.bfloat16)

    def write(s, value):
        value = jnp.where(owner != 0, value, jnp.zeros_like(value))
        fits[place_of(slots, is_a, s)] = value

    @pl.when(middle != 0)
    def _():
        copies = []
        for kind, field, distance, source, start, size, row in plan["moves"]:
            low, high = half - 1 - distance, half + distance
            slot = jnp.where((is_a != 0) == (kind == "near"), low, high)
            target = pert if field else dens
            copies.append(
                pltpu.make_async_copy(
                    ins[source].at[pl.ds(start, size)],
                    target.at[pl.ds(row, size), :, pl.ds(pl.multiple_of(slot * blk, blk), blk)],
                    sems.at[len(copies)],
                )
            )
        for copy in copies:
            copy.start()
        for copy in copies:
            copy.wait()
        in_groups(count_rows + 2 * half - 1, group, first_step)
        response_row(slots, keep, square, order, fit_row, write)


def second_kernel(slots, group, scal, keep, square, order, outs):
    def step(i):
        def write(s, value):
            outs[place_of(slots, scal[1], s), i] = value

        response_row(slots, keep, square, order, i, write)

    @pl.when(scal[0] != 0)
    def _():
        in_groups(outs.shape[1], group, step)


def pack_kernel(pattern, density_in, field_terms, near, far, flags, sems):
    slots, rows = pattern.shape
    half = slots // 2
    my_slot = lax.axis_index("orb")
    first_row = lax.axis_index("aux") * rows
    near_field = jnp.where(my_slot < half, 0, 1)
    copies = [
        pltpu.make_async_copy(pattern, flags, sems.at[0]),
        pltpu.make_async_copy(density_in.at[:, 0], near.at[pl.ds(0, rows)], sems.at[1]),
        pltpu.make_async_copy(density_in.at[:, 0], far.at[pl.ds(0, rows)], sems.at[2]),
        pltpu.make_async_copy(field_terms.at[near_field, :, 0], near.at[pl.ds(rows, rows)], sems.at[3]),
        pltpu.make_async_copy(field_terms.at[1 - near_field, :, 0], far.at[pl.ds(rows, rows)], sems.at[4]),
    ]
    for copy in copies:
        copy.start()
    for copy in copies:
        copy.wait()
    total_rows = lax.axis_size("aux") * rows
    for row in range(rows):
        column = first_row + row + my_slot - half
        kept = (flags[my_slot, row] == 1) & (column >= 0) & (column < total_rows)

        @pl.when(jnp.logical_not(kept))
        def _(row=row):
            for piece in (near, far):
                for place in (row, rows + row):
                    piece[place] = jnp.zeros_like(piece[place])


def preload_kernel(parts, *refs):
    refs, sems = refs[:-1], refs[-1]
    copies = []
    for source, row, rows, column, columns, target, target_row in parts:
        copies.append(
            pltpu.make_async_copy(
                refs[source].at[pl.ds(row, rows), pl.ds(column, columns)],
                refs[target].at[pl.ds(target_row, rows)],
                sems.at[len(copies)],
            )
        )
    for copy in copies:
        copy.start()
    for copy in copies:
        copy.wait()


def sums_kernel(pieces, place, *refs):
    pieces, integrals, out = refs[:pieces], refs[pieces:-1], refs[-1]
    pairs = pieces[0][...]
    for piece in pieces[1:]:
        pairs = pairs + piece[...]
    out[...] = jnp.zeros_like(out)
    fields = pairs.shape[0]
    flat = pairs.reshape(fields, -1)
    start = 0
    for part in integrals:
        width = part.shape[1]
        folds = flat.shape[1] // width
        rows = part.shape[0] // folds
        lhs = [flat[:, fold * width : (fold + 1) * width] for fold in range(folds)]
        lhs = lhs[0] if folds == 1 else jnp.concatenate(lhs, 0)
        value = lax.dot_general(
            lhs, part[...], (((1,), (1,)), ((), ())), preferred_element_type=jnp.float32
        )
        total = value[:fields, :rows]
        for fold in range(1, folds):
            total = total + value[fold * fields : (fold + 1) * fields, fold * rows : (fold + 1) * rows]
        out[place[0], :, start : start + rows] = total
        start += rows


def metric_kernel(place, *refs):
    pieces, (metric, out, sums) = refs[:-3], refs[-3:]
    for index, piece in enumerate(pieces):
        for core in range(2):
            sums[jnp.bitwise_xor(place[0], 2 * index) + core] = piece[core]
    groups, fields, width = sums.shape
    lanes = 128
    totals = [jnp.zeros((out.shape[1], lanes), jnp.float32) for _ in range(fields)]
    full = [
        jnp.concatenate([sums[group, field : field + 1, :] for group in range(groups)], 1)
        for field in range(fields)
    ]
    for start in range(0, groups * width, lanes):
        tile = metric[:, start : start + lanes]
        for field in range(fields):
            totals[field] = totals[field] + tile * full[field][:, start : start + lanes]
    for field in range(fields):
        out[field, :] = jnp.sum(totals[field].T, axis=0)


def on_device(band_pattern, density_in, field_terms, fit_blocks, tensor, metric_inv):
    count_rows = density_in.shape[0]
    blk = density_in.shape[-1]
    fields = field_terms.shape[0]
    slots = lax.axis_size("orb")
    half = slots // 2
    aux_count = lax.axis_size("aux")
    total_rows = count_rows * aux_count
    my_aux = lax.axis_index("aux")
    my_slot = lax.axis_index("orb")
    first_row = my_aux * count_rows
    side_a, side_b = half - 1, half
    is_a = my_slot < half
    middle = (my_slot == side_a) | (my_slot == side_b)
    zero_half = jnp.zeros((), jnp.bfloat16)
    up_rows, down_rows = 2 * half, 2 * half - 2
    forward = [
        (i * slots + side, (i + 1) * slots + side) for i in range(aux_count - 1) for side in (side_a, side_b)
    ]
    backward = [(target, source) for source, target in forward]

    near, far = pl.pallas_call(
        pack_kernel,
        out_shape=[jax.ShapeDtypeStruct((2 * count_rows, blk, blk), jnp.bfloat16)] * 2,
        in_specs=[pl.BlockSpec(memory_space=pltpu.HBM)] * 3,
        out_specs=[VMEM] * 2,
        scratch_shapes=[pltpu.SMEM((slots, count_rows), jnp.int32), pltpu.SemaphoreType.DMA((5,))],
        compiler_params=pltpu.CompilerParams(vmem_limit_bytes=4 << 20),
        name="pack",
    )(
        *(
            pltpu.with_memory_space_constraint(value, pltpu.HBM)
            for value in (band_pattern.T, density_in, field_terms)
        ),
    )

    inputs, moves = [], []

    def stage_rims(pieces, extra=None):
        split = lambda rows: (rows[:count_rows], rows[count_rows:])
        low = [part[count_rows - up_rows :] for _, _, rows in pieces for part in split(rows)]
        high = [part[:down_rows] for _, _, rows in pieces for part in split(rows)]
        if extra is not None:
            low, high = low + [extra], high + [extra]
        low = lax.ppermute(jnp.concatenate(low, 0), ("aux", "orb"), forward)
        high = lax.ppermute(jnp.concatenate(high, 0), ("aux", "orb"), backward)
        for source, size, row in ((low, up_rows, 0), (high, down_rows, up_rows + count_rows)):
            for index, (kind, distance, _) in enumerate(pieces):
                for field in range(2):
                    start = (2 * index + field) * size
                    moves.append((kind, field, distance, len(inputs), start, size, row))
            inputs.append(source)
        for kind, distance, rows in pieces:
            for field in range(2):
                moves.append((kind, field, distance, len(inputs), field * count_rows, count_rows, up_rows))
            inputs.append(rows)
        return low, high

    wanted = [(my_slot - side_a) % slots, (side_b - my_slot) % slots]
    wanted += [my_slot ^ plane for plane in range(slots)]
    wanted = [[index == step for step in range(slots)] for index in wanted]

    near_got, far_got = {0: near}, {}
    for distance in range(half):
        if distance:
            near_got[distance] = lax.ppermute(near, "orb", [(side_a - distance, side_a), (side_b + distance, side_b)])
        far_got[distance] = lax.ppermute(
            far, "orb", [(side_a - distance, side_b), (side_b + distance, side_a)]
        )
    pattern = jnp.pad(
        band_pattern.astype(jnp.bfloat16), ((0, blk - count_rows), (0, blk - slots))
    )[None]
    low, high = stage_rims([("near", 0, near)], pattern)
    core = my_aux.astype(jnp.int32) % 2
    source, metric_source, core, first_core, *flags = lax.optimization_barrier(
        [tensor, metric_inv, core[None], (my_aux.astype(jnp.int32) - core)[None]] + [flag for group in wanted for flag in group]
    )
    wanted = [flags[index : index + slots] for index in range(0, len(flags), slots)]
    source, metric_source = (
        pltpu.with_memory_space_constraint(value, pltpu.HBM)
        for value in (source.reshape(tensor.shape[1], -1), metric_source[0])
    )
    aux_rows, length = source.shape
    whole_rows = aux_rows // 256 * 256
    rest_rows = aux_rows - whole_rows
    folds = 2 if rest_rows <= 128 else 1

    def preload(sources, shapes, parts):
        held = pl.pallas_call(
            functools.partial(preload_kernel, parts),
            out_shape=shapes,
            in_specs=[pl.BlockSpec(memory_space=pltpu.HBM)] * len(sources),
            out_specs=[VMEM] * len(shapes),
            scratch_shapes=[pltpu.SemaphoreType.DMA((len(parts),))],
            compiler_params=pltpu.CompilerParams(vmem_limit_bytes=4 << 20),
        )(*sources)
        return [pltpu.with_memory_space_constraint(value, pltpu.VMEM) for value in held]

    def strips(index, start, rows, column, columns, target, target_row):
        count = max(count for count in (1, 2, 4, 8) if rows % (16 * count) == 0)
        height = rows // count
        return [
            (index, start + strip * height, height, column, columns, target, target_row + strip * height)
            for strip in range(count)
        ]

    integrals = []
    if whole_rows:
        integrals += preload(
            [source],
            [jax.ShapeDtypeStruct((whole_rows, length), source.dtype)],
            strips(0, 0, whole_rows, 0, length, 1, 0),
        )
    (metric,) = preload(
        [metric_source],
        [jax.ShapeDtypeStruct(metric_source.shape, metric_source.dtype)],
        strips(0, 0, metric_source.shape[0], 0, metric_source.shape[1], 1, 0),
    )
    if rest_rows:
        width = length // folds
        parts = []
        for fold in range(folds):
            parts += strips(0, whole_rows, rest_rows, fold * width, width, 1, fold * rest_rows)
        integrals += preload([source], [jax.ShapeDtypeStruct((folds * rest_rows, width), source.dtype)], parts)
    pattern_low = low[-1, count_rows - half : count_rows, :slots].astype(jnp.int32)
    pattern_high = high[-1, : half - 1, :slots].astype(jnp.int32)
    for distance in range(1, half):
        stage_rims(
            [("near", distance, near_got[distance]), ("far", distance - 1, far_got[distance - 1])]
        )
    stage_rims([("far", half - 1, far_got[half - 1])])

    pattern_wide = jnp.concatenate([pattern_low, band_pattern, pattern_high], 0)
    keep_wide = band_keep(pattern_wide, first_row - half, total_rows).astype(jnp.int32)
    owner = fit_blocks[0] // count_rows == my_aux
    scal = jnp.stack(
        [middle.astype(jnp.int32), is_a.astype(jnp.int32), fit_blocks[0] % count_rows, owner.astype(jnp.int32)]
    )
    wide_rows = count_rows + up_rows + down_rows
    mid_rows = count_rows + 2 * half - 1
    plan = {"inputs": len(inputs), "moves": tuple(moves)}
    group = mid_rows if slots <= 4 else 1
    bands = jax.ShapeDtypeStruct((mid_rows, blk, slots * blk), jnp.bfloat16)
    wide_band = pltpu.VMEM((wide_rows, blk, slots * blk), jnp.bfloat16)
    blocks = 2 * wide_rows * slots
    square, order, fit_parts = pl.pallas_call(
        functools.partial(first_kernel, slots, count_rows, group, plan),
        out_shape=[bands, bands, jax.ShapeDtypeStruct((slots, blk, blk), jnp.bfloat16)],
        in_specs=[SMEM, SMEM] + [ANY] * len(inputs),
        out_specs=[VMEM] * 3,
        scratch_shapes=[wide_band, wide_band, pltpu.SemaphoreType.DMA((len(moves),))],
        compiler_params=pltpu.CompilerParams(vmem_limit_bytes=blocks * blk * blk * 2 + (4 << 20)),
        name="mid_products",
    )(scal, keep_wide, *inputs)
    square, order = (pltpu.with_memory_space_constraint(value, pltpu.VMEM) for value in (square, order))
    parts = pl.pallas_call(
        functools.partial(second_kernel, slots, group),
        out_shape=jax.ShapeDtypeStruct((slots, count_rows, blk, blk), jnp.bfloat16),
        in_specs=[SMEM, SMEM, VMEM, VMEM],
        out_specs=VMEM,
        compiler_params=pltpu.CompilerParams(vmem_limit_bytes=4 << 20),
        name="mid_second",
    )(scal, keep_wide, square, order)

    def scatter(blocks):
        got = [blocks[0]]
        for step in range(1, slots):
            pairs = [(side_a, (side_a + step) % slots), (side_b, (side_b - step) % slots)]
            got.append(lax.ppermute(blocks[step], "orb", pairs))
        return got

    def assemble(got):
        picked = []
        for flags in wanted[:fields]:
            value = got[0]
            for step in range(1, slots):
                value = jnp.where(flags[step], got[step], value)
            picked.append(value)
        return jnp.stack(picked, 0)

    fit_own = assemble(scatter(fit_parts))
    got = scatter(parts)
    response = assemble(got)[:, :, None]
    fit_own = fit_own + lax.ppermute(fit_own, "aux", swap_pairs(aux_count, 1))
    fit_pieces = [fit_own] + [
        lax.ppermute(fit_own, "aux", swap_pairs(aux_count, distance)) for distance in range(2, aux_count, 2)
    ]

    sums = pl.pallas_call(
        functools.partial(sums_kernel, len(fit_pieces)),
        out_shape=jax.ShapeDtypeStruct((2, fields, aux_rows), jnp.float32),
        in_specs=[SMEM] + [VMEM] * (len(fit_pieces) + len(integrals)),
        out_specs=VMEM,
        compiler_params=pltpu.CompilerParams(vmem_limit_bytes=8 << 20),
        name="fit_sums",
    )(core, *fit_pieces, *integrals)
    sums = sums + lax.ppermute(sums, "aux", swap_pairs(aux_count, 1))
    pieces = [sums] + [
        lax.ppermute(sums, "aux", swap_pairs(aux_count, distance)) for distance in range(2, aux_count, 2)
    ]
    part = pl.pallas_call(
        metric_kernel,
        out_shape=jax.ShapeDtypeStruct((fields, metric.shape[0]), jnp.float32),
        in_specs=[SMEM] + [VMEM] * (len(pieces) + 1),
        out_specs=VMEM,
        scratch_shapes=[pltpu.VMEM((aux_count, fields, aux_rows), jnp.float32)],
        compiler_params=pltpu.CompilerParams(vmem_limit_bytes=8 << 20),
        name="metric",
    )(first_core, *pieces, metric)
    got = [part] * slots
    for distance in range(slots - 1, 0, -1):
        got[distance] = lax.ppermute(part, "orb", swap_pairs(slots, distance))
    coefficients = None
    for plane in range(slots):
        value = got[0]
        for distance in range(1, slots):
            value = jnp.where(wanted[fields + plane][distance], got[distance], value)
        coefficients = value if coefficients is None else coefficients + value
    return (response, coefficients[None])


def solution(mesh):
    in_specs = (
        P("aux", None),
        P("aux", "orb", None, None),
        P(None, "aux", "orb", None, None),
        P(),
        P(None, "aux", "orb", None),
        P(None, "aux", None),
    )
    out_specs = (P(None, "aux", "orb", None, None), P(None, None, "aux"))

    return jax.shard_map(on_device, mesh=mesh, in_specs=in_specs, out_specs=out_specs, check_vma=False)
```
